32 devices in a mesh: pop: 8 (over z, x), mp: 4 (over y, core).
Axes of the slice: x: 2, y: 2, z: 4, core: 2. Of those that a mesh axis runs over, the one named last changes fastest.
Arguments:
- context: bfloat16 [3072, 5120], P('pop', 'mp'), may hold values from -9 to 9
- out_weight: bfloat16 [5120, 5120], P('mp'), may hold values from -0.078125 to 0.078125
- residual: bfloat16 [3072, 5120], P('pop', 'mp'), may hold values from -6 to 6
- target: bfloat16 [3072, 5120], P('pop', 'mp'), may hold values from -9 to 9
- norm_gain: float32 [5120], replicated, may hold values from 0.5 to 1.5
- left_factors: bfloat16 [128, 5120], P('pop'), may hold values from -6 to 6
- right_factors: bfloat16 [128, 5120], P('pop'), may hold values from -8 to 8
- member_ranks: int32 [128], P('pop'), may hold values from 0 to 127, each once
Outputs:
- update: float32 [5120, 5120], P('pop', 'mp')
- fitness: float32 [128], P('pop')
- base: float32 [3072, 5120], P('pop', 'mp')
The draws below stay inside these ranges and needn't reach their ends.
Inputs may be any that keep to these rules, and one draw needn't show every extreme that they name: `member_ranks`: each number from 0 to 127 appears exactly once.
All inputs are finite; a program needn't handle non-finite values.
Results may differ from the reference program's by a relative error of at most 0.0095.
Values may be sent and summed in bfloat16 or wider, within the bound.
A program may use at most 64 MiB of HBM per device.

```python
import math
import jax
import jax.numpy as jnp
from jax import lax

D = 5120
TOK = 384
MEM_DEV = 16
MEMBERS = 128
TOKENS = 3072
N_POP = 8
N_MP = 4


def stream_draw(key):
    normal_part = jax.random.normal(jax.random.fold_in(key, 11), (TOKENS, D), jnp.float32)
    return jnp.clip(normal_part, -6.0, 6.0)


def shared_direction(key, salt):
    vector = jax.random.normal(jax.random.fold_in(key, salt), (1, D), jnp.float32)
    return jnp.clip(vector, -4.0, 4.0)


def draw_residual(key, part):
    return stream_draw(key).astype(jnp.bfloat16)


def draw_context(key, part):
    normal_part = jnp.clip(jax.random.normal(jax.random.fold_in(key, 33), (TOKENS, D), jnp.float32), -6.0, 6.0)
    common = shared_direction(key, 31)
    return jnp.clip(normal_part + 0.7 * common, -9.0, 9.0).astype(jnp.bfloat16)


def draw_right_factors(key, part):
    normal_part = jnp.clip(jax.random.normal(jax.random.fold_in(key, 34), (MEMBERS, D), jnp.float32), -6.0, 6.0)
    flips = jax.random.bernoulli(jax.random.fold_in(key, 35), 0.5, (MEMBERS, 1)).astype(jnp.float32)
    member_sign = 2.0 * flips - 1.0
    common = shared_direction(key, 32)
    return jnp.clip(normal_part + 0.5 * member_sign * common, -8.0, 8.0).astype(jnp.bfloat16)


def draw_target(key, part):
    stream = stream_draw(key)
    jitter = jax.random.normal(jax.random.fold_in(key, 12), (TOKENS, D), jnp.float32)
    mixed = stream + 0.2 * jnp.clip(jitter, -6.0, 6.0)
    normed = mixed / jnp.sqrt(jnp.mean(mixed * mixed, axis=1, keepdims=True) + 1e-06)
    noise = 0.3 * jnp.clip(jax.random.normal(jax.random.fold_in(key, 13), (TOKENS, D), jnp.float32), -6.0, 6.0)
    common = shared_direction(key, 32)
    return jnp.clip(normed + noise + 0.5 * common, -9.0, 9.0).astype(jnp.bfloat16)


def level_of(stream_key, dims, shards, smallest, largest):
    def one(position, shards_of):
        steps = jax.random.uniform(jax.random.fold_in(jax.random.fold_in(stream_key, 6), position), (shards_of,), jnp.float32, smallest / len(shards), largest / len(shards))
        return jnp.repeat(jnp.exp(steps), dims[position] // shards_of).reshape((-1,) + (1,) * (len(dims) - position - 1))

    gain = one(*shards[0])
    for cut in shards[1:]:
        gain = gain * one(*cut)
    return gain


def scatter_about(rng, extent, deviation, bound, pieces=(), kind=jnp.bfloat16):
    drawn = deviation * jax.random.normal(rng, extent, jnp.float32)
    if pieces:
        drawn = drawn * level_of(rng, extent, pieces, -0.22, 0.18)
    return jnp.clip(drawn, -bound, bound).astype(kind)


def setup_inputs(seed: int = 0) -> dict:
    keys = jax.random.split(jax.random.key(seed), 9)
    return {
        "context": draw_context(jax.random.fold_in(keys[8], 71), 0),
        "out_weight": scatter_about(keys[1], (D, D), D ** -0.5, 0.078125, ((0, 4),)),
        "residual": draw_residual(jax.random.fold_in(keys[8], 71), 0),
        "target": draw_target(jax.random.fold_in(keys[8], 71), 0),
        "norm_gain": jnp.clip(1.0 + 0.1 * jax.random.normal(keys[4], (D,), jnp.float32), 0.5, 1.5),
        "left_factors": scatter_about(keys[5], (MEMBERS, D), 1.0, 6.0, ((0, 8),)),
        "right_factors": draw_right_factors(jax.random.fold_in(keys[8], 71), 0),
        "member_ranks": jax.random.permutation(keys[7], MEMBERS).astype(jnp.int32),
    }


SIGMA = 1.0
EPSILON = 1e-06

def member_errors(stream, right_rows, projected, norm_gain, target_rows):
    factor = SIGMA / math.sqrt(D)
    hidden = stream[:, None, :] + factor * projected[:, :, None] * right_rows[None, :, :]
    meansq = lax.optimization_barrier(jnp.mean(hidden * hidden, axis=2, keepdims=True))
    normed = norm_gain * hidden * lax.rsqrt(meansq + EPSILON)
    differ = normed - target_rows[:, None, :]
    return lax.optimization_barrier(jnp.sum(differ * differ, axis=2))

def utility(member_ranks, count_all):
    levels = jnp.arange(count_all).astype(jnp.float32)
    ceiling = math.log(count_all / 2 + 1)
    baseline = jnp.maximum(0.0, ceiling - jnp.log(levels + 1.0))
    shaped = jnp.maximum(0.0, ceiling - jnp.log(member_ranks.astype(jnp.float32) + 1.0))
    return shaped / jnp.sum(baseline) - 1.0 / count_all

def reference(context, out_weight, residual, target, norm_gain, left_factors, right_factors, member_ranks):
    shard_width = D // N_MP
    stream = residual.astype(jnp.float32)
    for block in range(N_MP):
        offset = block * shard_width
        partial_value = jnp.dot(context[:, offset:offset + shard_width], out_weight[offset:offset + shard_width], preferred_element_type=jnp.float32)
        stream = stream + lax.optimization_barrier(partial_value.astype(jnp.bfloat16)).astype(jnp.float32)

    def scored(grouped):
        context_group, stream_group, target_group, left_group, right_group = grouped
        projected = lax.dot_general(context_group, left_group, (((1,), (1,)), ((), ())), preferred_element_type=jnp.float32)
        errors = member_errors(stream_group, right_group.astype(jnp.float32), projected, norm_gain, target_group.astype(jnp.float32))
        return -lax.optimization_barrier(jnp.sum(errors, axis=0)) / (TOK * D)
    fitness = lax.map(scored, (context.reshape(N_POP, TOK, D), stream.reshape(N_POP, TOK, D), target.reshape(N_POP, TOK, D), left_factors.reshape(N_POP, MEM_DEV, D), right_factors.reshape(N_POP, MEM_DEV, D))).reshape(MEMBERS)
    centre = fitness - jnp.mean(fitness)
    spread = jnp.sqrt(jnp.mean(centre * centre) + 1e-05)
    weight = utility(member_ranks, MEMBERS) + centre / spread / MEMBERS
    weighted = (weight[:, None] * left_factors.astype(jnp.float32)).astype(jnp.bfloat16)
    update = lax.dot_general(weighted, right_factors, (((0,), (0,)), ((), ())), preferred_element_type=jnp.float32) * (math.sqrt(MEMBERS) / SIGMA)
    return (update, fitness, stream)
```

```python
import functools
import math

import jax
import jax.numpy as jnp
from jax import lax
from jax.experimental import pallas as pl
from jax.experimental.pallas import tpu as pltpu
from jax.sharding import PartitionSpec as P

SIGMA = 1.0
EPSILON = 1e-06


def error_sums(stream, lifted, right_rows, gain_part, target_rows, inverse):
    hidden = stream[:, None, :] + lifted[:, :, None] * right_rows[None, :, :]
    differ = gain_part * hidden * inverse[:, :, None] - target_rows[:, None, :]
    return jnp.sum(differ * differ, axis=(0, 2))


def utility(member_ranks, count_all):
    levels = jnp.arange(count_all).astype(jnp.float32)
    ceiling = math.log(count_all / 2 + 1)
    baseline = jnp.maximum(0.0, ceiling - jnp.log(levels + 1.0))
    shaped = jnp.maximum(0.0, ceiling - jnp.log(member_ranks.astype(jnp.float32) + 1.0))
    return shaped / jnp.sum(baseline) - 1.0 / count_all


def shards(
    context, out_weight, residual, target, norm_gain, left_factors, right_factors, member_ranks
):
    tok_count = context.shape[0]
    shard_width = context.shape[1]
    full_width = out_weight.shape[1]
    factor = SIGMA / math.sqrt(full_width)
    offset = lax.axis_index("mp") * shard_width
    left_cols = lax.dynamic_slice_in_dim(left_factors, offset, shard_width, 1)
    right_cols = lax.dynamic_slice_in_dim(right_factors, offset, shard_width, 1)
    partial_value = jnp.dot(context, out_weight, preferred_element_type=jnp.float32)
    projected = lax.dot_general(
        context, left_cols, (((1,), (1,)), ((), ())), preferred_element_type=jnp.float32
    )
    summed = lax.psum_scatter(
        partial_value.astype(jnp.bfloat16), "mp", scatter_dimension=1, tiled=True
    ).astype(jnp.float32)
    stream = residual.astype(jnp.float32) + summed
    gain_part = lax.dynamic_slice_in_dim(norm_gain, offset, shard_width, 0)
    factor_f = right_cols.astype(jnp.float32)
    crossed = jnp.dot(stream, factor_f.T, precision=lax.Precision.HIGHEST)
    per_token = jnp.sum(stream * stream, axis=1)
    per_member = jnp.sum(factor_f * factor_f, axis=1)
    projected, crossed, per_token, per_member = lax.psum(
        (projected, crossed, per_token, per_member), "mp"
    )
    lifted = factor * projected
    meansq = (
        per_token[:, None] + 2.0 * lifted * crossed + lifted * lifted * per_member[None, :]
    ) / full_width
    inverse = lax.rsqrt(meansq + EPSILON)
    local_error = error_sums(
        stream, lifted, factor_f, gain_part, target.astype(jnp.float32), inverse
    )
    member_total = lax.psum(local_error, "mp")
    fitness = -member_total / (tok_count * full_width)
    everyone = lax.all_gather(fitness, "pop", axis=0, tiled=True)
    count_all = everyone.shape[0]
    average = jnp.mean(everyone)
    centre = everyone - average
    spread = jnp.sqrt(jnp.mean(centre * centre) + 1e-05)
    weight = utility(member_ranks, count_all) + (fitness - average) / spread / count_all
    weighted = (weight[:, None] * left_factors.astype(jnp.float32)).astype(jnp.bfloat16)
    weighted_rows = lax.all_to_all(weighted, "pop", split_axis=1, concat_axis=0, tiled=True)
    right_all = lax.all_gather(right_cols, "pop", axis=0, tiled=True)
    update = lax.dot_general(
        weighted_rows, right_all, (((0,), (0,)), ((), ())), preferred_element_type=jnp.float32
    ) * (math.sqrt(count_all) / SIGMA)
    return (update, fitness, stream)


BLK = 256
F32 = jnp.float32
BF = jnp.bfloat16


def nt_dot(a, b):
    return lax.dot_general(a, b, (((1,), (1,)), ((), ())), preferred_element_type=F32)


def split_two(x):
    hi = x.astype(BF)
    return hi, (x - hi.astype(F32)).astype(BF)


def row_sums(ones, acc):
    hi = acc.astype(BF)
    rest = acc - hi.astype(F32)
    mid, low = split_two(rest)
    return nt_dot(ones, hi) + nt_dot(ones, mid) + nt_dot(ones, low)


def fold_lanes(x):
    total = x[:, :128]
    for i in range(1, x.shape[1] // 128):
        total = total + x[:, i * 128:(i + 1) * 128]
    return total


def kernel(
    n_pop, n_mp, ctx_h, w_h, res_h, tgt_h, gain, left_h, right_h, right, ranks,
    base, weighted, right_all, fit_out,
    w_v, ctx, res, tgt, lcols, send_a, recv_a, send_y, recv_y, send_b, recv_b,
    lall, rall, uall, mixed, sq_s, sq_a, sq_e, pre, pre_in, post, post_in, part_m, fits,
    w_sem, loc_sem, sa, ra, sy, ry, sb, rb, s_pre, r_pre, s_post, r_post, s_m, r_m,
    s_l, r_l, s_r, r_r, s_u, r_u, s_f, r_f,
):
    tok, width = ctx.shape
    mem = right.shape[0]
    full = right.shape[1]
    rows = full // n_pop
    chunks = width // BLK
    quarter = tok // n_mp
    members = mem * n_pop
    p = lax.axis_index("pop")
    q = lax.axis_index("mp")
    y = q // 2
    c = q % 2
    mate = y * 2 + (1 - c)
    across = (1 - y) * 2 + c
    diagonal = (1 - y) * 2 + (1 - c)
    blocks = (diagonal, across, mate, q)

    def remote(src, dst, ss, rs, pop, mp):
        return pltpu.make_async_remote_copy(
            src_ref=src, dst_ref=dst, send_sem=ss, recv_sem=rs,
            device_id=(pop, mp), device_id_type=pl.DeviceIdType.MESH,
        )

    def w_copy(s, k):
        start = pl.multiple_of(blocks[s] * width + k * BLK, BLK)
        return pltpu.make_async_copy(w_h.at[:, pl.ds(start, BLK)], w_v.at[s, k], w_sem.at[s, k])

    my_cols = pl.ds(pl.multiple_of(q * width, BLK), width)
    my_rows = pl.ds(pl.multiple_of(p * rows, 128), rows)
    locals_ = [
        pltpu.make_async_copy(ctx_h, ctx, loc_sem.at[0]),
        pltpu.make_async_copy(res_h, res, loc_sem.at[1]),
        pltpu.make_async_copy(tgt_h, tgt, loc_sem.at[2]),
        pltpu.make_async_copy(left_h.at[:, my_cols], lcols, loc_sem.at[3]),
        pltpu.make_async_copy(left_h.at[:, my_rows], lall.at[0], loc_sem.at[4]),
        pltpu.make_async_copy(right_h.at[:, my_cols], rall.at[0], loc_sem.at[5]),
    ]
    locals_[0].start()
    for k in range(chunks):
        w_copy(0, k).start()
        w_copy(1, k).start()
    for k in range(chunks):
        w_copy(2, k).start()
        w_copy(3, k).start()
    for item in locals_[1:]:
        item.start()

    barrier = pltpu.get_barrier_semaphore()
    for d in range(1, n_mp):
        pl.semaphore_signal(barrier, inc=1, device_id=(p, (q + d) % n_mp), device_id_type=pl.DeviceIdType.MESH)
    for d in range(1, n_pop):
        pl.semaphore_signal(barrier, inc=1, device_id=((p + d) % n_pop, q), device_id_type=pl.DeviceIdType.MESH)
    pl.semaphore_wait(barrier, n_mp - 1 + n_pop - 1)

    def copy_a(k):
        return remote(send_a.at[k], recv_a.at[k], sa.at[k], ra.at[k], p, mate)

    def copy_y(k):
        return remote(send_y.at[k], recv_y.at[k], sy.at[k], ry.at[k], p, across)

    def copy_b(k):
        return remote(send_b.at[k], recv_b.at[k], sb.at[k], rb.at[k], p, mate)

    def copy_l(d):
        peer = (p + d) % n_pop
        cols = pl.ds(pl.multiple_of(peer * rows, 128), rows)
        return remote(left_h.at[:, cols], lall.at[d], s_l.at[d - 1], r_l.at[d - 1], peer, q)

    def copy_r(d):
        return remote(right_h.at[:, my_cols], rall.at[d], s_r.at[d - 1], r_r.at[d - 1], (p + d) % n_pop, q)

    def copy_u(d):
        return remote(ranks, uall.at[d], s_u.at[d - 1], r_u.at[d - 1], (p + d) % n_pop, q)

    def copy_f(d):
        return remote(fits.at[0], fits.at[d], s_f.at[d - 1], r_f.at[d - 1], (p + d) % n_pop, q)

    def copy_pre(d):
        peer = (q + d) % n_mp
        return remote(pre.at[peer], pre_in.at[d - 1], s_pre.at[d - 1], r_pre.at[d - 1], p, peer)

    def copy_post(d):
        peer = (q + d) % n_mp
        return remote(post.at[peer], post_in.at[d - 1], s_post.at[d - 1], r_post.at[d - 1], p, peer)

    def copy_m(d):
        return remote(part_m.at[q], part_m.at[q], s_m.at[d - 1], r_m.at[d - 1], p, (q + d) % n_mp)

    def arrive_m(d):
        source = (q + n_mp - d) % n_mp
        return remote(part_m.at[source], part_m.at[source], s_m.at[d - 1], r_m.at[d - 1], p, source)

    locals_[0].wait()

    def far(k, carry):
        w_copy(0, k).wait()
        send_a[k] = jnp.dot(ctx[...], w_v[0, k], preferred_element_type=F32).astype(BF)
        copy_a(k).start()
        w_copy(1, k).wait()
        mine = jnp.dot(ctx[...], w_v[1, k], preferred_element_type=F32)
        copy_a(k).wait_recv()
        send_y[k] = (mine + recv_a[k].astype(F32)).astype(BF)
        copy_y(k).start()
        return carry

    lax.fori_loop(0, chunks, far, 0)

    for d in range(1, n_pop):
        copy_l(d).start()
        copy_r(d).start()
        copy_u(d).start()

    for item in locals_[1:]:
        item.wait()

    def near(k, carry):
        w_copy(2, k).wait()
        send_b[k] = jnp.dot(ctx[...], w_v[2, k], preferred_element_type=F32).astype(BF)
        copy_b(k).start()
        w_copy(3, k).wait()
        cols = pl.ds(pl.multiple_of(k * BLK, BLK), BLK)
        base[:, cols] = jnp.dot(ctx[...], w_v[3, k], preferred_element_type=F32) + res[:, cols].astype(F32)
        return carry

    lax.fori_loop(0, chunks, near, 0)

    ones = jnp.ones((8, 128), BF)
    gain_mine = gain[:, my_cols]
    r_mine = rall[0].astype(F32)
    gr_hi, gr_lo = split_two(r_mine * gain_mine)
    for t in range(n_mp):
        part = slice(t * quarter, (t + 1) * quarter)
        target = tgt[part, :]
        pre[t, 0:mem, :] = nt_dot(lcols[...], ctx[part, :])
        pre[t, mem:2 * mem, :] = nt_dot(gr_hi, target) + nt_dot(gr_lo, target)
        wide = target.astype(F32)
        pre[t, 2 * mem:2 * mem + 8, :] = row_sums(ones, fold_lanes(wide * wide))
    for d in range(1, n_mp):
        copy_pre(d).start()
    g2_hi, g2_lo = split_two(r_mine * (gain_mine * gain_mine))
    for k in range(chunks):
        cols = slice(k * BLK, (k + 1) * BLK)
        mixed[k, 0:mem, :] = rall[0, :, cols]
        mixed[k, mem:2 * mem, :] = g2_hi[:, cols]
        mixed[k, 2 * mem:3 * mem, :] = g2_lo[:, cols]
    r_full = right[...].astype(F32)
    gr_full = r_full * gain[...]
    norm_r = jnp.sum(r_full * r_full, axis=1, keepdims=True)
    norm_gr = jnp.sum(gr_full * gr_full, axis=1, keepdims=True)
    sq_s[...] = jnp.zeros_like(sq_s)
    sq_a[...] = jnp.zeros_like(sq_a)
    sq_e[...] = jnp.zeros_like(sq_e)
    post[...] = jnp.zeros_like(post)
    uall[0] = ranks[...]

    def settle(k, carry):
        copy_b(k).wait_recv()
        copy_y(k).wait_recv()
        cols = pl.ds(pl.multiple_of(k * BLK, BLK), BLK)
        gain_k = gain[:, pl.ds(pl.multiple_of(q * width + k * BLK, BLK), BLK)]
        for t in range(n_mp):
            part = slice(t * quarter, (t + 1) * quarter)
            s = base[part, cols] + recv_b[k, part, :].astype(F32) + recv_y[k, part, :].astype(F32)
            base[part, cols] = s
            hi, low = split_two(s)
            both = nt_dot(mixed[k], hi) + nt_dot(mixed[k], low)
            post[t, 0:mem, :] += both[0:mem]
            post[t, mem:2 * mem, :] += both[mem:2 * mem] + both[2 * mem:3 * mem]
            gs = s * gain_k
            sq_s[part, :] += fold_lanes(s * s)
            sq_a[part, :] += fold_lanes(gs * gs)
            sq_e[part, :] += fold_lanes(gs * tgt[part, cols].astype(F32))
        return carry

    lax.fori_loop(0, chunks, settle, 0)
    for t in range(n_mp):
        part = slice(t * quarter, (t + 1) * quarter)
        post[t, 2 * mem:2 * mem + 8, :] = row_sums(ones, sq_s[part, :])
        post[t, 2 * mem + 8:2 * mem + 16, :] = row_sums(ones, sq_a[part, :])
        post[t, 2 * mem + 16:2 * mem + 24, :] = row_sums(ones, sq_e[part, :])
    for d in range(1, n_mp):
        copy_post(d).start()
    early = pre[q]
    for d in range(1, n_mp):
        copy_pre(d).wait_recv()
        early = early + pre_in[d - 1]
    late = post[q]
    for d in range(1, n_mp):
        copy_post(d).wait_recv()
        late = late + post_in[d - 1]
    lifted = early[0:mem] * (SIGMA / math.sqrt(full))
    cross_t = early[mem:2 * mem]
    t_sq = early[2 * mem:2 * mem + 1]
    crossed = late[0:mem]
    crossed_g = late[mem:2 * mem]
    s_sq = late[2 * mem:2 * mem + 1]
    a_sq = late[2 * mem + 8:2 * mem + 9]
    e_sq = late[2 * mem + 16:2 * mem + 17]
    meansq = (s_sq + 2.0 * lifted * crossed + lifted * lifted * norm_r) / full
    inverse = lax.rsqrt(meansq + EPSILON)
    power = a_sq + 2.0 * lifted * crossed_g + lifted * lifted * norm_gr
    errors = inverse * inverse * power - 2.0 * inverse * (e_sq + lifted * cross_t) + t_sq
    part_m[q] = jnp.broadcast_to(jnp.sum(errors, axis=1, keepdims=True), (mem, 128))
    for d in range(1, n_mp):
        copy_m(d).start()
    for d in range(1, n_mp):
        arrive_m(d).wait_recv()
    total = part_m[0]
    for i in range(1, n_mp):
        total = total + part_m[i]
    fitness = -total / (tok * full)
    fits[0] = fitness
    for d in range(1, n_pop):
        copy_f(d).start()
    fit_out[...] = fitness
    for d in range(1, n_pop):
        copy_l(d).wait_recv()
        copy_r(d).wait_recv()
        copy_u(d).wait_recv()
    right_all[...] = rall[...]
    ceiling = math.log(members / 2 + 1)
    whole = sum(max(0.0, ceiling - math.log(i + 1.0)) for i in range(members))
    shaped = jnp.maximum(0.0, ceiling - jnp.log(uall[...] + 1.0)) / whole - 1.0 / members
    for d in range(1, n_pop):
        copy_f(d).wait_recv()
    everyone = fits[...]
    average = jnp.sum(jnp.sum(everyone, axis=0), axis=0, keepdims=True) / members
    centre = everyone - average[None]
    spread = jnp.sqrt(jnp.sum(jnp.sum(centre * centre, axis=0), axis=0, keepdims=True) / members + 1e-05)
    weight = shaped + centre / spread[None] / members
    for d in range(n_pop):
        for i in range(rows // 128):
            cols = slice(i * 128, (i + 1) * 128)
            weighted[d, :, cols] = (weight[d] * lall[d, :, cols].astype(F32)).astype(BF)

    def drain(k, carry):
        copy_a(k).wait_send()
        copy_y(k).wait_send()
        copy_b(k).wait_send()
        return carry

    lax.fori_loop(0, chunks, drain, 0)
    for d in range(1, n_mp):
        copy_pre(d).wait_send()
        copy_post(d).wait_send()
        copy_m(d).wait_send()
    for d in range(1, n_pop):
        copy_l(d).wait_send()
        copy_r(d).wait_send()
        copy_u(d).wait_send()
        copy_f(d).wait_send()


def fused_shards(
    n_pop, n_mp, context, out_weight, residual, target, norm_gain, left_factors, right_factors, member_ranks
):
    tok, width = context.shape
    full = out_weight.shape[1]
    mem = left_factors.shape[0]
    rows = full // n_pop
    chunks = width // BLK
    quarter = tok // n_mp
    ranks = jnp.broadcast_to(member_ranks.astype(F32)[:, None], (mem, 128))
    anywhere = pl.BlockSpec(memory_space=pltpu.HBM)
    vmem = pl.BlockSpec(memory_space=pltpu.VMEM)
    block = pltpu.VMEM((chunks, tok, BLK), BF)
    dma = pltpu.SemaphoreType.DMA
    acc = pltpu.VMEM((tok, 128), F32)
    base, weighted, right_all, fitness = pl.pallas_call(
        functools.partial(kernel, n_pop, n_mp),
        name="es_step",
        out_shape=(
            jax.ShapeDtypeStruct((tok, width), F32),
            jax.ShapeDtypeStruct((n_pop, mem, rows), BF),
            jax.ShapeDtypeStruct((n_pop, mem, width), BF),
            jax.ShapeDtypeStruct((mem, 128), F32),
        ),
        in_specs=[anywhere] * 4 + [vmem, anywhere, anywhere, vmem, vmem],
        out_specs=[vmem] * 4,
        scratch_shapes=[
            pltpu.VMEM((4, chunks, width, BLK), BF),
            pltpu.VMEM((tok, width), BF),
            pltpu.VMEM((tok, width), BF),
            pltpu.VMEM((tok, width), BF),
            pltpu.VMEM((mem, width), BF),
            block, block, block, block, block, block,
            pltpu.VMEM((n_pop, mem, rows), BF),
            pltpu.VMEM((n_pop, mem, width), BF),
            pltpu.VMEM((n_pop, mem, 128), F32),
            pltpu.VMEM((chunks, 3 * mem, BLK), BF),
            acc, acc, acc,
            pltpu.VMEM((n_mp, 2 * mem + 8, quarter), F32),
            pltpu.VMEM((n_mp - 1, 2 * mem + 8, quarter), F32),
            pltpu.VMEM((n_mp, 2 * mem + 24, quarter), F32),
            pltpu.VMEM((n_mp - 1, 2 * mem + 24, quarter), F32),
            pltpu.VMEM((n_mp, mem, 128), F32),
            pltpu.VMEM((n_pop, mem, 128), F32),
            dma((4, chunks)),
            dma((6,)),
        ]
        + [dma((chunks,))] * 6
        + [dma((n_mp - 1,))] * 6
        + [dma((n_pop - 1,))] * 8,
        compiler_params=pltpu.CompilerParams(
            collective_id=0, has_side_effects=True, vmem_limit_bytes=48 * 1024 * 1024
        ),
    )(
        context, out_weight, residual, target, norm_gain.reshape(1, full), left_factors,
        right_factors, right_factors, ranks,
    )
    count_all = n_pop * mem
    update = lax.dot_general(
        weighted.reshape(count_all, rows), right_all.reshape(count_all, width),
        (((0,), (0,)), ((), ())), preferred_element_type=F32,
    ) * (math.sqrt(count_all) / SIGMA)
    return (update, fitness[:, 0], base)


def chosen(n_pop, n_mp, context, out_weight, *rest):
    tok, width = context.shape
    mem = rest[3].shape[0]
    full = out_weight.shape[1]
    if n_mp == 4 and width % BLK == 0 and (full // n_pop) % 128 == 0 and tok % (16 * n_mp) == 0 and mem % 16 == 0:
        return fused_shards(n_pop, n_mp, context, out_weight, *rest)
    return shards(context, out_weight, *rest)


def solution(mesh):
    in_specs = (
        P("pop", "mp"),
        P("mp", None),
        P("pop", "mp"),
        P("pop", "mp"),
        P(),
        P("pop", None),
        P("pop", None),
        P("pop"),
    )
    out_specs = (P("pop", "mp"), P("pop"), P("pop", "mp"))
    return jax.shard_map(
        functools.partial(chosen, mesh.shape["pop"], mesh.shape["mp"]), mesh=mesh, in_specs=in_specs, out_specs=out_specs, check_vma=False)
```

```python
import functools
import math

import jax
import jax.numpy as jnp
from jax import lax
from jax.experimental import pallas as pl
from jax.experimental.pallas import tpu as pltpu
from jax.sharding import PartitionSpec as P

SIGMA = 1.0
EPSILON = 1e-06


def error_sums(stream, lifted, right_rows, gain_part, target_rows, inverse):
    hidden = stream[:, None, :] + lifted[:, :, None] * right_rows[None, :, :]
    differ = gain_part * hidden * inverse[:, :, None] - target_rows[:, None, :]
    return jnp.sum(differ * differ, axis=(0, 2))


def utility(member_ranks, count_all):
    levels = jnp.arange(count_all).astype(jnp.float32)
    ceiling = math.log(count_all / 2 + 1)
    baseline = jnp.maximum(0.0, ceiling - jnp.log(levels + 1.0))
    shaped = jnp.maximum(0.0, ceiling - jnp.log(member_ranks.astype(jnp.float32) + 1.0))
    return shaped / jnp.sum(baseline) - 1.0 / count_all


def shards(
    context, out_weight, residual, target, norm_gain, left_factors, right_factors, member_ranks
):
    tok_count = context.shape[0]
    shard_width = context.shape[1]
    full_width = out_weight.shape[1]
    factor = SIGMA / math.sqrt(full_width)
    offset = lax.axis_index("mp") * shard_width
    left_cols = lax.dynamic_slice_in_dim(left_factors, offset, shard_width, 1)
    right_cols = lax.dynamic_slice_in_dim(right_factors, offset, shard_width, 1)
    partial_value = jnp.dot(context, out_weight, preferred_element_type=jnp.float32)
    projected = lax.dot_general(
        context, left_cols, (((1,), (1,)), ((), ())), preferred_element_type=jnp.float32
    )
    summed = lax.psum_scatter(
        partial_value.astype(jnp.bfloat16), "mp", scatter_dimension=1, tiled=True
    ).astype(jnp.float32)
    stream = residual.astype(jnp.float32) + summed
    gain_part = lax.dynamic_slice_in_dim(norm_gain, offset, shard_width, 0)
    factor_f = right_cols.astype(jnp.float32)
    crossed = jnp.dot(stream, factor_f.T, precision=lax.Precision.HIGHEST)
    per_token = jnp.sum(stream * stream, axis=1)
    per_member = jnp.sum(factor_f * factor_f, axis=1)
    projected, crossed, per_token, per_member = lax.psum(
        (projected, crossed, per_token, per_member), "mp"
    )
    lifted = factor * projected
    meansq = (
        per_token[:, None] + 2.0 * lifted * crossed + lifted * lifted * per_member[None, :]
    ) / full_width
    inverse = lax.rsqrt(meansq + EPSILON)
    local_error = error_sums(
        stream, lifted, factor_f, gain_part, target.astype(jnp.float32), inverse
    )
    member_total = lax.psum(local_error, "mp")
    fitness = -member_total / (tok_count * full_width)
    everyone = lax.all_gather(fitness, "pop", axis=0, tiled=True)
    count_all = everyone.shape[0]
    average = jnp.mean(everyone)
    centre = everyone - average
    spread = jnp.sqrt(jnp.mean(centre * centre) + 1e-05)
    weight = utility(member_ranks, count_all) + (fitness - average) / spread / count_all
    weighted = (weight[:, None] * left_factors.astype(jnp.float32)).astype(jnp.bfloat16)
    weighted_rows = lax.all_to_all(weighted, "pop", split_axis=1, concat_axis=0, tiled=True)
    right_all = lax.all_gather(right_cols, "pop", axis=0, tiled=True)
    update = lax.dot_general(
        weighted_rows, right_all, (((0,), (0,)), ((), ())), preferred_element_type=jnp.float32
    ) * (math.sqrt(count_all) / SIGMA)
    return (update, fitness, stream)


BLK = 256
F32 = jnp.float32
BF = jnp.bfloat16


def nt_dot(a, b):
    return lax.dot_general(a, b, (((1,), (1,)), ((), ())), preferred_element_type=F32)


def split_two(x):
    hi = x.astype(BF)
    return hi, (x - hi.astype(F32)).astype(BF)


def row_sums(ones, acc):
    hi = acc.astype(BF)
    rest = acc - hi.astype(F32)
    mid, low = split_two(rest)
    return nt_dot(ones, hi) + nt_dot(ones, mid) + nt_dot(ones, low)


def fold_lanes(x):
    total = x[:, :128]
    for i in range(1, x.shape[1] // 128):
        total = total + x[:, i * 128:(i + 1) * 128]
    return total


def kernel(
    n_pop, n_mp, ctx_h, w_h, res_h, tgt_h, gain, left_h, right_h, right, ranks,
    base, weighted, right_all, fit_out,
    w_v, ctx, res, tgt, lcols, send_a, recv_a, send_y, recv_y, send_b, recv_b,
    lall, rall, uall, mixed, sq_s, sq_a, sq_e, pre, pre_in, post, post_in, part_m, fits,
    w_sem, loc_sem, sa, ra, sy, ry, sb, rb, s_pre, r_pre, s_post, r_post, s_m, r_m,
    s_l, r_l, s_r, r_r, s_u, r_u, s_f, r_f,
):
    tok, width = ctx.shape
    mem = right.shape[0]
    full = right.shape[1]
    rows = full // n_pop
    chunks = width // BLK
    quarter = tok // n_mp
    members = mem * n_pop
    p = lax.axis_index("pop")
    q = lax.axis_index("mp")
    y = q // 2
    c = q % 2
    mate = y * 2 + (1 - c)
    across = (1 - y) * 2 + c
    diagonal = (1 - y) * 2 + (1 - c)
    blocks = (diagonal, across, mate, q)

    def remote(src, dst, ss, rs, pop, mp):
        return pltpu.make_async_remote_copy(
            src_ref=src, dst_ref=dst, send_sem=ss, recv_sem=rs,
            device_id=(pop, mp), device_id_type=pl.DeviceIdType.MESH,
        )

    def w_copy(s, k):
        start = pl.multiple_of(blocks[s] * width + k * BLK, BLK)
        return pltpu.make_async_copy(w_h.at[:, pl.ds(start, BLK)], w_v.at[s, k], w_sem.at[s, k])

    my_cols = pl.ds(pl.multiple_of(q * width, BLK), width)
    my_rows = pl.ds(pl.multiple_of(p * rows, 128), rows)
    locals_ = [
        pltpu.make_async_copy(ctx_h, ctx, loc_sem.at[0]),
        pltpu.make_async_copy(res_h, res, loc_sem.at[1]),
        pltpu.make_async_copy(tgt_h, tgt, loc_sem.at[2]),
        pltpu.make_async_copy(left_h.at[:, my_cols], lcols, loc_sem.at[3]),
        pltpu.make_async_copy(left_h.at[:, my_rows], lall.at[0], loc_sem.at[4]),
        pltpu.make_async_copy(right_h.at[:, my_cols], rall.at[0], loc_sem.at[5]),
    ]
    locals_[0].start()
    for k in range(chunks):
        for s in range(3):
            w_copy(s, k).start()
    for k in range(chunks):
        w_copy(3, k).start()
    for item in locals_[1:]:
        item.start()

    barrier = pltpu.get_barrier_semaphore()
    for d in range(1, n_mp):
        pl.semaphore_signal(barrier, inc=1, device_id=(p, (q + d) % n_mp), device_id_type=pl.DeviceIdType.MESH)
    for d in range(1, n_pop):
        pl.semaphore_signal(barrier, inc=1, device_id=((p + d) % n_pop, q), device_id_type=pl.DeviceIdType.MESH)
    pl.semaphore_wait(barrier, n_mp - 1 + n_pop - 1)

    def copy_a(k):
        return remote(send_a.at[k], recv_a.at[k], sa.at[k], ra.at[k], p, mate)

    def copy_y(k):
        return remote(send_y.at[k], recv_y.at[k], sy.at[k], ry.at[k], p, across)

    def copy_b(k):
        return remote(send_b.at[k], recv_b.at[k], sb.at[k], rb.at[k], p, mate)

    def copy_l(d):
        peer = (p + d) % n_pop
        cols = pl.ds(pl.multiple_of(peer * rows, 128), rows)
        return remote(left_h.at[:, cols], lall.at[d], s_l.at[d - 1], r_l.at[d - 1], peer, q)

    def copy_r(d):
        return remote(right_h.at[:, my_cols], rall.at[d], s_r.at[d - 1], r_r.at[d - 1], (p + d) % n_pop, q)

    def copy_u(d):
        return remote(uall.at[0], uall.at[d], s_u.at[d - 1], r_u.at[d - 1], (p + d) % n_pop, q)

    def copy_f(d):
        return remote(fits.at[0], fits.at[d], s_f.at[d - 1], r_f.at[d - 1], (p + d) % n_pop, q)

    def copy_pre(d):
        peer = (q + d) % n_mp
        return remote(pre.at[peer], pre_in.at[d - 1], s_pre.at[d - 1], r_pre.at[d - 1], p, peer)

    def copy_post(d):
        peer = (q + d) % n_mp
        return remote(post.at[peer], post_in.at[d - 1], s_post.at[d - 1], r_post.at[d - 1], p, peer)

    def copy_m(d):
        return remote(part_m.at[q], part_m.at[q], s_m.at[d - 1], r_m.at[d - 1], p, (q + d) % n_mp)

    def arrive_m(d):
        source = (q + n_mp - d) % n_mp
        return remote(part_m.at[source], part_m.at[source], s_m.at[d - 1], r_m.at[d - 1], p, source)

    locals_[0].wait()

    def far(k, carry):
        w_copy(0, k).wait()
        send_a[k] = jnp.dot(ctx[...], w_v[0, k], preferred_element_type=F32).astype(BF)
        copy_a(k).start()
        w_copy(1, k).wait()
        mine = jnp.dot(ctx[...], w_v[1, k], preferred_element_type=F32)
        w_copy(2, k).wait()
        send_b[k] = jnp.dot(ctx[...], w_v[2, k], preferred_element_type=F32).astype(BF)
        copy_b(k).start()
        copy_a(k).wait_recv()
        send_y[k] = (mine + recv_a[k].astype(F32)).astype(BF)
        copy_y(k).start()
        return carry

    lax.fori_loop(0, chunks, far, 0)

    uall[0] = ranks[...].astype(F32)
    for d in range(1, n_pop):
        copy_l(d).start()
        copy_r(d).start()
        copy_u(d).start()

    for item in locals_[1:]:
        item.wait()

    def near(k, carry):
        w_copy(3, k).wait()
        cols = pl.ds(pl.multiple_of(k * BLK, BLK), BLK)
        base[:, cols] = jnp.dot(ctx[...], w_v[3, k], preferred_element_type=F32) + res[:, cols].astype(F32)
        return carry

    lax.fori_loop(0, chunks, near, 0)

    ones = jnp.ones((8, 128), BF)
    gain_mine = gain[:, my_cols]
    r_mine = rall[0].astype(F32)
    gr_hi, gr_lo = split_two(r_mine * gain_mine)
    for t in range(n_mp):
        part = slice(t * quarter, (t + 1) * quarter)
        target = tgt[part, :]
        pre[t, 0:mem, :] = nt_dot(lcols[...], ctx[part, :])
        pre[t, mem:2 * mem, :] = nt_dot(gr_hi, target) + nt_dot(gr_lo, target)
        wide = target.astype(F32)
        pre[t, 2 * mem:2 * mem + 8, :] = row_sums(ones, fold_lanes(wide * wide))
    for d in range(1, n_mp):
        copy_pre(d).start()
    g2_hi, g2_lo = split_two(r_mine * (gain_mine * gain_mine))
    for k in range(chunks):
        cols = slice(k * BLK, (k + 1) * BLK)
        mixed[k, 0:mem, :] = rall[0, :, cols]
        mixed[k, mem:2 * mem, :] = g2_hi[:, cols]
        mixed[k, 2 * mem:3 * mem, :] = g2_lo[:, cols]
    r_full = right[...].astype(F32)
    gr_full = r_full * gain[...]
    norm_r = jnp.sum(r_full * r_full, axis=1, keepdims=True)
    norm_gr = jnp.sum(gr_full * gr_full, axis=1, keepdims=True)
    sq_s[...] = jnp.zeros_like(sq_s)
    sq_a[...] = jnp.zeros_like(sq_a)
    sq_e[...] = jnp.zeros_like(sq_e)
    post[...] = jnp.zeros_like(post)

    def settle(k, carry):
        copy_b(k).wait_recv()
        copy_y(k).wait_recv()
        cols = pl.ds(pl.multiple_of(k * BLK, BLK), BLK)
        gain_k = gain[:, pl.ds(pl.multiple_of(q * width + k * BLK, BLK), BLK)]
        for t in range(n_mp):
            part = slice(t * quarter, (t + 1) * quarter)
            s = base[part, cols] + recv_b[k, part, :].astype(F32) + recv_y[k, part, :].astype(F32)
            base[part, cols] = s
            hi, low = split_two(s)
            both = nt_dot(mixed[k], hi) + nt_dot(mixed[k], low)
            post[t, 0:mem, :] += both[0:mem]
            post[t, mem:2 * mem, :] += both[mem:2 * mem] + both[2 * mem:3 * mem]
            gs = s * gain_k
            sq_s[part, :] += fold_lanes(s * s)
            sq_a[part, :] += fold_lanes(gs * gs)
            sq_e[part, :] += fold_lanes(gs * tgt[part, cols].astype(F32))
        return carry

    lax.fori_loop(0, chunks, settle, 0)
    line = lax.broadcasted_iota(jnp.int32, (8, quarter), 0)
    for t in range(n_mp):
        part = slice(t * quarter, (t + 1) * quarter)
        rest = jnp.where(line == 1, row_sums(ones, sq_a[part, :]), row_sums(ones, sq_e[part, :]))
        post[t, 2 * mem:2 * mem + 8, :] = jnp.where(line == 0, row_sums(ones, sq_s[part, :]), rest)
    for d in range(1, n_mp):
        copy_post(d).start()
    early = pre[q]
    for d in range(1, n_mp):
        copy_pre(d).wait_recv()
        early = early + pre_in[d - 1]
    late = post[q]
    for d in range(1, n_mp):
        copy_post(d).wait_recv()
        late = late + post_in[d - 1]
    lifted = early[0:mem] * (SIGMA / math.sqrt(full))
    cross_t = early[mem:2 * mem]
    t_sq = early[2 * mem:2 * mem + 1]
    crossed = late[0:mem]
    crossed_g = late[mem:2 * mem]
    s_sq = late[2 * mem:2 * mem + 1]
    a_sq = late[2 * mem + 1:2 * mem + 2]
    e_sq = late[2 * mem + 2:2 * mem + 3]
    meansq = (s_sq + 2.0 * lifted * crossed + lifted * lifted * norm_r) / full
    inverse = lax.rsqrt(meansq + EPSILON)
    power = a_sq + 2.0 * lifted * crossed_g + lifted * lifted * norm_gr
    errors = inverse * inverse * power - 2.0 * inverse * (e_sq + lifted * cross_t) + t_sq
    part_m[q] = row_sums(jnp.ones((8, quarter), BF), errors)[0:1]
    for d in range(1, n_mp):
        copy_m(d).start()
    for d in range(1, n_mp):
        arrive_m(d).wait_recv()
    total = part_m[0]
    for i in range(1, n_mp):
        total = total + part_m[i]
    fitness = -total / (tok * full)
    fits[0] = fitness
    for d in range(1, n_pop):
        copy_f(d).start()
    fit_out[...] = fitness
    for d in range(1, n_pop):
        copy_l(d).wait_recv()
        copy_r(d).wait_recv()
        copy_u(d).wait_recv()
    for d in range(n_pop):
        right_all[d * mem:(d + 1) * mem, :] = rall[d]
    ceiling = math.log(members / 2 + 1)
    whole = sum(max(0.0, ceiling - math.log(i + 1.0)) for i in range(members))
    shaped = jnp.maximum(0.0, ceiling - jnp.log(uall[...] + 1.0)) / whole - 1.0 / members
    for d in range(1, n_pop):
        copy_f(d).wait_recv()
    everyone = fits[...]
    average = jnp.sum(jnp.sum(everyone, axis=0), axis=1, keepdims=True) / members
    centre = everyone - average[None]
    spread = jnp.sqrt(jnp.sum(jnp.sum(centre * centre, axis=0), axis=1, keepdims=True) / members + 1e-05)
    weight = shaped + centre / spread[None] / members
    square = (mem, mem)
    eye = lax.broadcasted_iota(jnp.int32, square, 0) == lax.broadcasted_iota(jnp.int32, square, 1)
    for d in range(n_pop):
        upright = jnp.sum(jnp.where(eye, weight[d], 0.0), axis=1, keepdims=True)
        weighted[d * mem:(d + 1) * mem, :] = (upright * lall[d].astype(F32)).astype(BF)

    def drain(k, carry):
        copy_a(k).wait_send()
        copy_y(k).wait_send()
        copy_b(k).wait_send()
        return carry

    lax.fori_loop(0, chunks, drain, 0)
    for d in range(1, n_mp):
        copy_pre(d).wait_send()
        copy_post(d).wait_send()
        copy_m(d).wait_send()
    for d in range(1, n_pop):
        copy_l(d).wait_send()
        copy_r(d).wait_send()
        copy_u(d).wait_send()
        copy_f(d).wait_send()


def in_hbm(x):
    return pltpu.with_memory_space_constraint(x, pltpu.HBM)


def fused_shards(
    n_pop, n_mp, context, out_weight, residual, target, norm_gain, left_factors, right_factors, member_ranks
):
    tok, width = context.shape
    full = out_weight.shape[1]
    mem = left_factors.shape[0]
    rows = full // n_pop
    chunks = width // BLK
    quarter = tok // n_mp
    ranks = member_ranks.reshape(1, mem)
    anywhere = pl.BlockSpec(memory_space=pltpu.HBM)
    vmem = pl.BlockSpec(memory_space=pltpu.VMEM)
    block = pltpu.VMEM((chunks, tok, BLK), BF)
    dma = pltpu.SemaphoreType.DMA
    acc = pltpu.VMEM((tok, 128), F32)
    base, weighted, right_all, fitness = pl.pallas_call(
        functools.partial(kernel, n_pop, n_mp),
        name="es_step",
        out_shape=(
            jax.ShapeDtypeStruct((tok, width), F32),
            jax.ShapeDtypeStruct((n_pop * mem, rows), BF),
            jax.ShapeDtypeStruct((n_pop * mem, width), BF),
            jax.ShapeDtypeStruct((1, mem), F32),
        ),
        in_specs=[anywhere] * 4 + [vmem, anywhere, anywhere, vmem, vmem],
        out_specs=[vmem] * 4,
        scratch_shapes=[
            pltpu.VMEM((4, chunks, width, BLK), BF),
            pltpu.VMEM((tok, width), BF),
            pltpu.VMEM((tok, width), BF),
            pltpu.VMEM((tok, width), BF),
            pltpu.VMEM((mem, width), BF),
            block, block, block, block, block, block,
            pltpu.VMEM((n_pop, mem, rows), BF),
            pltpu.VMEM((n_pop, mem, width), BF),
            pltpu.VMEM((n_pop, 1, mem), F32),
            pltpu.VMEM((chunks, 3 * mem, BLK), BF),
            acc, acc, acc,
            pltpu.VMEM((n_mp, 2 * mem + 8, quarter), F32),
            pltpu.VMEM((n_mp - 1, 2 * mem + 8, quarter), F32),
            pltpu.VMEM((n_mp, 2 * mem + 8, quarter), F32),
            pltpu.VMEM((n_mp - 1, 2 * mem + 8, quarter), F32),
            pltpu.VMEM((n_mp, 1, mem), F32),
            pltpu.VMEM((n_pop, 1, mem), F32),
            dma((4, chunks)),
            dma((6,)),
        ]
        + [dma((chunks,))] * 6
        + [dma((n_mp - 1,))] * 6
        + [dma((n_pop - 1,))] * 8,
        compiler_params=pltpu.CompilerParams(
            collective_id=0, has_side_effects=True, vmem_limit_bytes=48 * 1024 * 1024
        ),
    )(
        *map(in_hbm, (context, out_weight, residual, target)), norm_gain.reshape(1, full),
        in_hbm(left_factors), in_hbm(right_factors), right_factors, ranks,
    )
    count_all = n_pop * mem
    steps = rows // 128
    part = width // steps
    update, base, fitness = pl.pallas_call(
        functools.partial(finish, math.sqrt(count_all) / SIGMA),
        name="es_update",
        grid=(steps,),
        out_shape=(
            jax.ShapeDtypeStruct((rows, width), F32),
            jax.ShapeDtypeStruct((tok, width), F32),
            jax.ShapeDtypeStruct((1, mem), F32),
        ),
        in_specs=[
            pl.BlockSpec((count_all, 128), lambda i: (0, i)),
            pl.BlockSpec((count_all, width), lambda i: (0, 0)),
            pl.BlockSpec((tok, part), lambda i: (0, i)),
            pl.BlockSpec((1, mem), lambda i: (0, 0)),
        ],
        out_specs=(
            pl.BlockSpec((128, width), lambda i: (i, 0)),
            pl.BlockSpec((tok, part), lambda i: (0, i)),
            pl.BlockSpec((1, mem), lambda i: (0, 0)),
        ),
        compiler_params=pltpu.CompilerParams(vmem_limit_bytes=16 * 1024 * 1024),
    )(weighted, right_all, base, fitness)
    return (update, fitness.reshape(mem), base)


def finish(scale, weighted, right_all, base_in, fit_in, update, base, fit):
    update[...] = lax.dot_general(
        weighted[...], right_all[...], (((0,), (0,)), ((), ())), preferred_element_type=F32
    ) * scale
    base[...] = base_in[...]
    fit[...] = fit_in[...]


def chosen(n_pop, n_mp, context, out_weight, *rest):
    tok, width = context.shape
    mem = rest[3].shape[0]
    full = out_weight.shape[1]
    full_rows = full // n_pop
    if n_mp == 4 and width % BLK == 0 and (full // n_pop) % 128 == 0 and tok % (16 * n_mp) == 0 and mem % 16 == 0 and width % full_rows == 0:
        return fused_shards(n_pop, n_mp, context, out_weight, *rest)
    return shards(context, out_weight, *rest)


def solution(mesh):
    in_specs = (
        P("pop", "mp"),
        P("mp", None),
        P("pop", "mp"),
        P("pop", "mp"),
        P(),
        P("pop", None),
        P("pop", None),
        P("pop"),
    )
    out_specs = (P("pop", "mp"), P("pop"), P("pop", "mp"))
    return jax.shard_map(
        functools.partial(chosen, mesh.shape["pop"], mesh.shape["mp"]), mesh=mesh, in_specs=in_specs, out_specs=out_specs, check_vma=False)
```

```python
import functools
import math

import jax
import jax.numpy as jnp
from jax import lax
from jax.experimental import pallas as pl
from jax.experimental.pallas import tpu as pltpu
from jax.sharding import PartitionSpec as P

SIGMA = 1.0
EPSILON = 1e-06


def error_sums(stream, lifted, right_rows, gain_part, target_rows, inverse):
    hidden = stream[:, None, :] + lifted[:, :, None] * right_rows[None, :, :]
    differ = gain_part * hidden * inverse[:, :, None] - target_rows[:, None, :]
    return jnp.sum(differ * differ, axis=(0, 2))


def utility(member_ranks, count_all):
    levels = jnp.arange(count_all).astype(jnp.float32)
    ceiling = math.log(count_all / 2 + 1)
    baseline = jnp.maximum(0.0, ceiling - jnp.log(levels + 1.0))
    shaped = jnp.maximum(0.0, ceiling - jnp.log(member_ranks.astype(jnp.float32) + 1.0))
    return shaped / jnp.sum(baseline) - 1.0 / count_all


def shards(
    context, out_weight, residual, target, norm_gain, left_factors, right_factors, member_ranks
):
    tok_count = context.shape[0]
    shard_width = context.shape[1]
    full_width = out_weight.shape[1]
    factor = SIGMA / math.sqrt(full_width)
    offset = lax.axis_index("mp") * shard_width
    left_cols = lax.dynamic_slice_in_dim(left_factors, offset, shard_width, 1)
    right_cols = lax.dynamic_slice_in_dim(right_factors, offset, shard_width, 1)
    partial_value = jnp.dot(context, out_weight, preferred_element_type=jnp.float32)
    projected = lax.dot_general(
        context, left_cols, (((1,), (1,)), ((), ())), preferred_element_type=jnp.float32
    )
    summed = lax.psum_scatter(
        partial_value.astype(jnp.bfloat16), "mp", scatter_dimension=1, tiled=True
    ).astype(jnp.float32)
    stream = residual.astype(jnp.float32) + summed
    gain_part = lax.dynamic_slice_in_dim(norm_gain, offset, shard_width, 0)
    factor_f = right_cols.astype(jnp.float32)
    crossed = jnp.dot(stream, factor_f.T, precision=lax.Precision.HIGHEST)
    per_token = jnp.sum(stream * stream, axis=1)
    per_member = jnp.sum(factor_f * factor_f, axis=1)
    projected, crossed, per_token, per_member = lax.psum(
        (projected, crossed, per_token, per_member), "mp"
    )
    lifted = factor * projected
    meansq = (
        per_token[:, None] + 2.0 * lifted * crossed + lifted * lifted * per_member[None, :]
    ) / full_width
    inverse = lax.rsqrt(meansq + EPSILON)
    local_error = error_sums(
        stream, lifted, factor_f, gain_part, target.astype(jnp.float32), inverse
    )
    member_total = lax.psum(local_error, "mp")
    fitness = -member_total / (tok_count * full_width)
    everyone = lax.all_gather(fitness, "pop", axis=0, tiled=True)
    count_all = everyone.shape[0]
    average = jnp.mean(everyone)
    centre = everyone - average
    spread = jnp.sqrt(jnp.mean(centre * centre) + 1e-05)
    weight = utility(member_ranks, count_all) + (fitness - average) / spread / count_all
    weighted = (weight[:, None] * left_factors.astype(jnp.float32)).astype(jnp.bfloat16)
    weighted_rows = lax.all_to_all(weighted, "pop", split_axis=1, concat_axis=0, tiled=True)
    right_all = lax.all_gather(right_cols, "pop", axis=0, tiled=True)
    update = lax.dot_general(
        weighted_rows, right_all, (((0,), (0,)), ((), ())), preferred_element_type=jnp.float32
    ) * (math.sqrt(count_all) / SIGMA)
    return (update, fitness, stream)


BLK = 256
F32 = jnp.float32
BF = jnp.bfloat16


def nt_dot(a, b):
    return lax.dot_general(a, b, (((1,), (1,)), ((), ())), preferred_element_type=F32)


def split_two(x):
    hi = x.astype(BF)
    return hi, (x - hi.astype(F32)).astype(BF)


def row_sums(ones, acc):
    hi = acc.astype(BF)
    rest = acc - hi.astype(F32)
    mid, low = split_two(rest)
    return nt_dot(ones, hi) + nt_dot(ones, mid) + nt_dot(ones, low)


def fold_lanes(x):
    total = x[:, :128]
    for i in range(1, x.shape[1] // 128):
        total = total + x[:, i * 128:(i + 1) * 128]
    return total


def kernel(
    n_pop, n_mp, ctx_h, w_h, res_h, tgt_h, gain_h, left_h, right_h, ranks_h,
    base, weighted, right_all, fit_out,
    w_v, ctx, res, tgt, lcols, gain, right, ranks, send_a, recv_a, send_y, recv_y, send_b, recv_b,
    lall, rall, uall, mixed, sq_s, sq_a, sq_e, pre, pre_in, post, post_in, fits,
    w_sem, loc_sem, sa, ra, sy, ry, sb, rb, s_pre, r_pre, s_post, r_post,
    s_l, r_l, s_r, r_r, s_u, r_u, s_f, r_f,
):
    tok, width = ctx.shape
    mem = right.shape[0]
    full = right.shape[1]
    rows = full // n_pop
    chunks = width // BLK
    quarter = tok // n_mp
    members = mem * n_pop
    p = lax.axis_index("pop")
    q = lax.axis_index("mp")
    y = q // 2
    c = q % 2
    mate = y * 2 + (1 - c)
    across = (1 - y) * 2 + c
    diagonal = (1 - y) * 2 + (1 - c)
    blocks = (diagonal, across, mate, q)

    def remote(src, dst, ss, rs, pop, mp):
        return pltpu.make_async_remote_copy(
            src_ref=src, dst_ref=dst, send_sem=ss, recv_sem=rs,
            device_id=(pop, mp), device_id_type=pl.DeviceIdType.MESH,
        )

    def w_copy(s, k):
        start = pl.multiple_of(blocks[s] * width + k * BLK, BLK)
        return pltpu.make_async_copy(w_h.at[:, pl.ds(start, BLK)], w_v.at[s, k], w_sem.at[s, k])

    my_cols = pl.ds(pl.multiple_of(q * width, BLK), width)
    my_rows = pl.ds(pl.multiple_of(p * rows, 128), rows)
    locals_ = [
        pltpu.make_async_copy(ctx_h, ctx, loc_sem.at[0]),
        pltpu.make_async_copy(res_h, res, loc_sem.at[1]),
        pltpu.make_async_copy(tgt_h, tgt, loc_sem.at[2]),
        pltpu.make_async_copy(left_h.at[:, my_cols], lcols, loc_sem.at[3]),
        pltpu.make_async_copy(left_h.at[:, my_rows], lall.at[0], loc_sem.at[4]),
        pltpu.make_async_copy(right_h.at[:, my_cols], rall.at[0], loc_sem.at[5]),
        pltpu.make_async_copy(gain_h, gain, loc_sem.at[6]),
        pltpu.make_async_copy(right_h, right, loc_sem.at[7]),
        pltpu.make_async_copy(ranks_h, ranks, loc_sem.at[8]),
    ]
    locals_[0].start()
    for k in range(2):
        for s in range(3):
            w_copy(s, k).start()

    barrier = pltpu.get_barrier_semaphore()
    peers = [(i, j) for i in range(n_pop) for j in range(n_mp)][1:]
    for i, j in peers:
        pl.semaphore_signal(
            barrier, inc=1, device_id=((p + i) % n_pop, (q + j) % n_mp), device_id_type=pl.DeviceIdType.MESH
        )

    def copy_a(k):
        return remote(send_a.at[k], recv_a.at[k], sa.at[k], ra.at[k], p, mate)

    def copy_y(k):
        return remote(send_y.at[k], recv_y.at[k], sy.at[k], ry.at[k], p, across)

    def copy_b(k):
        return remote(send_b.at[k], recv_b.at[k], sb.at[k], rb.at[k], p, mate)

    def copy_l(d):
        peer = (p + d) % n_pop
        cols = pl.ds(pl.multiple_of(peer * rows, 128), rows)
        return remote(left_h.at[:, cols], lall.at[d], s_l.at[d - 1], r_l.at[d - 1], peer, q)

    def copy_r(d):
        return remote(right_h.at[:, my_cols], rall.at[d], s_r.at[d - 1], r_r.at[d - 1], (p + d) % n_pop, q)

    def copy_u(d):
        return remote(uall.at[0], uall.at[d], s_u.at[d - 1], r_u.at[d - 1], (p + d) % n_pop, q)

    def copy_f(i, j):
        n = i * n_mp + j - 1
        return remote(fits.at[0, q], fits.at[i, q], s_f.at[n], r_f.at[n], (p + i) % n_pop, (q + j) % n_mp)

    def arrive_f(i, j):
        n = i * n_mp + j - 1
        source = (q + n_mp - j) % n_mp
        return remote(fits.at[i, source], fits.at[i, source], s_f.at[n], r_f.at[n], (p + n_pop - i) % n_pop, source)

    def copy_pre(d):
        peer = (q + d) % n_mp
        return remote(pre.at[peer], pre_in.at[d - 1], s_pre.at[d - 1], r_pre.at[d - 1], p, peer)

    def copy_post(d):
        peer = (q + d) % n_mp
        return remote(post.at[peer], post_in.at[d - 1], s_post.at[d - 1], r_post.at[d - 1], p, peer)

    def product(s, k):
        w_copy(s, k).wait()
        return jnp.dot(ctx[...], w_v[s, k], preferred_element_type=F32)

    locals_[0].wait()
    send_a[0] = product(0, 0).astype(BF)
    pl.semaphore_wait(barrier, n_mp * n_pop - 1)
    copy_a(0).start()

    def far(k, carry):
        @pl.when(k + 2 < chunks)
        def _():
            for s in range(3):
                w_copy(s, k + 2).start()

        w_copy(3, k).start()

        @pl.when(k == 1)
        def _():
            for item in locals_[1:]:
                item.start()

        mine = product(1, k)

        @pl.when(k + 1 < chunks)
        def _():
            send_a[k + 1] = product(0, k + 1).astype(BF)
            copy_a(k + 1).start()

        copy_a(k).wait_recv()
        send_y[k] = (mine + recv_a[k].astype(F32)).astype(BF)
        copy_y(k).start()
        send_b[k] = product(2, k).astype(BF)
        copy_b(k).start()
        return carry

    lax.fori_loop(0, chunks, far, 0)

    for item in locals_[1:]:
        item.wait()
    uall[0] = ranks[...].astype(F32)
    for d in range(1, n_pop):
        copy_l(d).start()
        copy_r(d).start()
        copy_u(d).start()

    def near(k, carry):
        cols = pl.ds(pl.multiple_of(k * BLK, BLK), BLK)
        base[:, cols] = product(3, k) + res[:, cols].astype(F32)
        return carry

    lax.fori_loop(0, chunks, near, 0)

    ones = jnp.ones((8, 128), BF)
    gain_mine = gain[:, my_cols]
    r_mine = rall[0].astype(F32)
    gr_hi, gr_lo = split_two(r_mine * gain_mine)
    for t in range(n_mp):
        part = slice(t * quarter, (t + 1) * quarter)
        target = tgt[part, :]
        pre[t, 0:mem, :] = nt_dot(lcols[...], ctx[part, :])
        pre[t, mem:2 * mem, :] = nt_dot(gr_hi, target) + nt_dot(gr_lo, target)
        wide = target.astype(F32)
        pre[t, 2 * mem:2 * mem + 8, :] = row_sums(ones, fold_lanes(wide * wide))
    for d in range(1, n_mp):
        copy_pre(d).start()
    g2_hi, g2_lo = split_two(r_mine * (gain_mine * gain_mine))
    for k in range(chunks):
        cols = slice(k * BLK, (k + 1) * BLK)
        mixed[k, 0:mem, :] = rall[0, :, cols]
        mixed[k, mem:2 * mem, :] = g2_hi[:, cols]
        mixed[k, 2 * mem:3 * mem, :] = g2_lo[:, cols]
    r_full = right[...].astype(F32)
    gr_full = r_full * gain[...]
    norm_r = jnp.sum(r_full * r_full, axis=1, keepdims=True)
    norm_gr = jnp.sum(gr_full * gr_full, axis=1, keepdims=True)
    sq_s[...] = jnp.zeros_like(sq_s)
    sq_a[...] = jnp.zeros_like(sq_a)
    sq_e[...] = jnp.zeros_like(sq_e)
    post[...] = jnp.zeros_like(post)

    def settle(k, carry):
        copy_b(k).wait_recv()
        copy_y(k).wait_recv()
        cols = pl.ds(pl.multiple_of(k * BLK, BLK), BLK)
        gain_k = gain[:, pl.ds(pl.multiple_of(q * width + k * BLK, BLK), BLK)]
        for t in range(n_mp):
            part = slice(t * quarter, (t + 1) * quarter)
            s = base[part, cols] + recv_b[k, part, :].astype(F32) + recv_y[k, part, :].astype(F32)
            base[part, cols] = s
            hi, low = split_two(s)
            both = nt_dot(mixed[k], hi) + nt_dot(mixed[k], low)
            post[t, 0:mem, :] += both[0:mem]
            post[t, mem:2 * mem, :] += both[mem:2 * mem] + both[2 * mem:3 * mem]
            gs = s * gain_k
            sq_s[part, :] += fold_lanes(s * s)
            sq_a[part, :] += fold_lanes(gs * gs)
            sq_e[part, :] += fold_lanes(gs * tgt[part, cols].astype(F32))
        return carry

    lax.fori_loop(0, chunks, settle, 0)
    line = lax.broadcasted_iota(jnp.int32, (8, quarter), 0)
    for t in range(n_mp):
        part = slice(t * quarter, (t + 1) * quarter)
        rest = jnp.where(line == 1, row_sums(ones, sq_a[part, :]), row_sums(ones, sq_e[part, :]))
        post[t, 2 * mem:2 * mem + 8, :] = jnp.where(line == 0, row_sums(ones, sq_s[part, :]), rest)
    for d in range(1, n_mp):
        copy_post(d).start()
    early = pre[q]
    for d in range(1, n_mp):
        copy_pre(d).wait_recv()
        early = early + pre_in[d - 1]
    late = post[q]
    for d in range(1, n_mp):
        copy_post(d).wait_recv()
        late = late + post_in[d - 1]
    lifted = early[0:mem] * (SIGMA / math.sqrt(full))
    cross_t = early[mem:2 * mem]
    t_sq = early[2 * mem:2 * mem + 1]
    crossed = late[0:mem]
    crossed_g = late[mem:2 * mem]
    s_sq = late[2 * mem:2 * mem + 1]
    a_sq = late[2 * mem + 1:2 * mem + 2]
    e_sq = late[2 * mem + 2:2 * mem + 3]
    meansq = (s_sq + 2.0 * lifted * crossed + lifted * lifted * norm_r) / full
    inverse = lax.rsqrt(meansq + EPSILON)
    power = a_sq + 2.0 * lifted * crossed_g + lifted * lifted * norm_gr
    errors = inverse * inverse * power - 2.0 * inverse * (e_sq + lifted * cross_t) + t_sq
    fits[0, q] = row_sums(jnp.ones((8, quarter), BF), errors)[0:1]
    for i, j in peers:
        copy_f(i, j).start()
    for d in range(1, n_pop):
        copy_l(d).wait_recv()
        copy_r(d).wait_recv()
        copy_u(d).wait_recv()
    for d in range(n_pop):
        right_all[d * mem:(d + 1) * mem, :] = rall[d]
    ceiling = math.log(members / 2 + 1)
    whole = sum(max(0.0, ceiling - math.log(i + 1.0)) for i in range(members))
    shaped = jnp.maximum(0.0, ceiling - jnp.log(uall[...] + 1.0)) / whole - 1.0 / members
    for i, j in peers:
        arrive_f(i, j).wait_recv()
    total = fits[:, 0]
    for j in range(1, n_mp):
        total = total + fits[:, j]
    everyone = -total / (tok * full)
    fit_out[...] = everyone[0]
    average = jnp.sum(jnp.sum(everyone, axis=0), axis=1, keepdims=True) / members
    centre = everyone - average[None]
    spread = jnp.sqrt(jnp.sum(jnp.sum(centre * centre, axis=0), axis=1, keepdims=True) / members + 1e-05)
    weight = shaped + centre / spread[None] / members
    square = (mem, mem)
    eye = lax.broadcasted_iota(jnp.int32, square, 0) == lax.broadcasted_iota(jnp.int32, square, 1)
    for d in range(n_pop):
        upright = jnp.sum(jnp.where(eye, weight[d], 0.0), axis=1, keepdims=True)
        weighted[d * mem:(d + 1) * mem, :] = (upright * lall[d].astype(F32)).astype(BF)

    def drain(k, carry):
        copy_a(k).wait_send()
        copy_y(k).wait_send()
        copy_b(k).wait_send()
        return carry

    lax.fori_loop(0, chunks, drain, 0)
    for d in range(1, n_mp):
        copy_pre(d).wait_send()
        copy_post(d).wait_send()
    for d in range(1, n_pop):
        copy_l(d).wait_send()
        copy_r(d).wait_send()
        copy_u(d).wait_send()
    for i, j in peers:
        copy_f(i, j).wait_send()


def in_hbm(x):
    return pltpu.with_memory_space_constraint(x, pltpu.HBM)


def fused_shards(
    n_pop, n_mp, context, out_weight, residual, target, norm_gain, left_factors, right_factors, member_ranks
):
    tok, width = context.shape
    full = out_weight.shape[1]
    mem = left_factors.shape[0]
    rows = full // n_pop
    chunks = width // BLK
    quarter = tok // n_mp
    ranks = member_ranks.reshape(1, mem)
    anywhere = pl.BlockSpec(memory_space=pltpu.HBM)
    vmem = pl.BlockSpec(memory_space=pltpu.VMEM)
    block = pltpu.VMEM((chunks, tok, BLK), BF)
    dma = pltpu.SemaphoreType.DMA
    acc = pltpu.VMEM((tok, 128), F32)
    base, weighted, right_all, fitness = pl.pallas_call(
        functools.partial(kernel, n_pop, n_mp),
        name="es_step",
        out_shape=(
            jax.ShapeDtypeStruct((tok, width), F32),
            jax.ShapeDtypeStruct((n_pop * mem, rows), BF),
            jax.ShapeDtypeStruct((n_pop * mem, width), BF),
            jax.ShapeDtypeStruct((1, mem), F32),
        ),
        in_specs=[anywhere] * 8,
        out_specs=[vmem] * 4,
        scratch_shapes=[
            pltpu.VMEM((4, chunks, width, BLK), BF),
            pltpu.VMEM((tok, width), BF),
            pltpu.VMEM((tok, width), BF),
            pltpu.VMEM((tok, width), BF),
            pltpu.VMEM((mem, width), BF),
            pltpu.VMEM((1, full), F32),
            pltpu.VMEM((mem, full), BF),
            pltpu.VMEM((1, mem), jnp.int32),
            block, block, block, block, block, block,
            pltpu.VMEM((n_pop, mem, rows), BF),
            pltpu.VMEM((n_pop, mem, width), BF),
            pltpu.VMEM((n_pop, 1, mem), F32),
            pltpu.VMEM((chunks, 3 * mem, BLK), BF),
            acc, acc, acc,
            pltpu.VMEM((n_mp, 2 * mem + 8, quarter), F32),
            pltpu.VMEM((n_mp - 1, 2 * mem + 8, quarter), F32),
            pltpu.VMEM((n_mp, 2 * mem + 8, quarter), F32),
            pltpu.VMEM((n_mp - 1, 2 * mem + 8, quarter), F32),
            pltpu.VMEM((n_pop, n_mp, 1, mem), F32),
            dma((4, chunks)),
            dma((9,)),
        ]
        + [dma((chunks,))] * 6
        + [dma((n_mp - 1,))] * 4
        + [dma((n_pop - 1,))] * 6
        + [dma((n_mp * n_pop - 1,))] * 2,
        compiler_params=pltpu.CompilerParams(
            collective_id=0, has_side_effects=True, vmem_limit_bytes=48 * 1024 * 1024
        ),
    )(
        *map(in_hbm, (
            context, out_weight, residual, target, norm_gain.reshape(1, full), left_factors,
            right_factors, ranks,
        ))
    )
    count_all = n_pop * mem
    update, base, fitness = pl.pallas_call(
        functools.partial(finish, math.sqrt(count_all) / SIGMA),
        name="es_update",
        out_shape=(
            jax.ShapeDtypeStruct((rows, width), F32),
            jax.ShapeDtypeStruct((tok, width), F32),
            jax.ShapeDtypeStruct((1, mem), F32),
        ),
        in_specs=[vmem] * 4,
        out_specs=[anywhere] * 3,
        scratch_shapes=[pltpu.VMEM((rows, width), F32), dma((rows // 128 + 2,))],
        compiler_params=pltpu.CompilerParams(vmem_limit_bytes=16 * 1024 * 1024),
    )(weighted, right_all, base, fitness)
    return (update, fitness.reshape(mem), base)


def finish(scale, weighted, right_all, base_in, fit_in, update, base, fit, held, sems):
    steps = held.shape[0] // 128
    copies = [
        pltpu.make_async_copy(base_in, base, sems.at[steps]),
        pltpu.make_async_copy(fit_in, fit, sems.at[steps + 1]),
    ]
    copies[0].start()
    copies[1].start()
    for i in range(steps):
        part = slice(i * 128, (i + 1) * 128)
        held[part, :] = lax.dot_general(
            weighted[:, part], right_all[...], (((0,), (0,)), ((), ())), preferred_element_type=F32
        ) * scale
        copies.append(pltpu.make_async_copy(held.at[part], update.at[part], sems.at[i]))
        copies[-1].start()
    for item in copies:
        item.wait()


def chosen(n_pop, n_mp, context, out_weight, *rest):
    tok, width = context.shape
    mem = rest[3].shape[0]
    full = out_weight.shape[1]
    if n_mp == 4 and width % BLK == 0 and width > BLK and (full // n_pop) % 128 == 0 and tok % (16 * n_mp) == 0 and mem % 16 == 0:
        return fused_shards(n_pop, n_mp, context, out_weight, *rest)
    return shards(context, out_weight, *rest)


def solution(mesh):
    in_specs = (
        P("pop", "mp"),
        P("mp", None),
        P("pop", "mp"),
        P("pop", "mp"),
        P(),
        P("pop", None),
        P("pop", None),
        P("pop"),
    )
    out_specs = (P("pop", "mp"), P("pop"), P("pop", "mp"))
    return jax.shard_map(
        functools.partial(chosen, mesh.shape["pop"], mesh.shape["mp"]), mesh=mesh, in_specs=in_specs, out_specs=out_specs, check_vma=False)
```

```python
import functools
import math

import jax
import jax.numpy as jnp
from jax import lax
from jax.experimental import pallas as pl
from jax.experimental.pallas import tpu as pltpu
from jax.sharding import PartitionSpec as P

SIGMA = 1.0
EPSILON = 1e-06


def error_sums(stream, lifted, right_rows, gain_part, target_rows, inverse):
    hidden = stream[:, None, :] + lifted[:, :, None] * right_rows[None, :, :]
    differ = gain_part * hidden * inverse[:, :, None] - target_rows[:, None, :]
    return jnp.sum(differ * differ, axis=(0, 2))


def utility(member_ranks, count_all):
    levels = jnp.arange(count_all).astype(jnp.float32)
    ceiling = math.log(count_all / 2 + 1)
    baseline = jnp.maximum(0.0, ceiling - jnp.log(levels + 1.0))
    shaped = jnp.maximum(0.0, ceiling - jnp.log(member_ranks.astype(jnp.float32) + 1.0))
    return shaped / jnp.sum(baseline) - 1.0 / count_all


def shards(
    context, out_weight, residual, target, norm_gain, left_factors, right_factors, member_ranks
):
    tok_count = context.shape[0]
    shard_width = context.shape[1]
    full_width = out_weight.shape[1]
    factor = SIGMA / math.sqrt(full_width)
    offset = lax.axis_index("mp") * shard_width
    left_cols = lax.dynamic_slice_in_dim(left_factors, offset, shard_width, 1)
    right_cols = lax.dynamic_slice_in_dim(right_factors, offset, shard_width, 1)
    partial_value = jnp.dot(context, out_weight, preferred_element_type=jnp.float32)
    projected = lax.dot_general(
        context, left_cols, (((1,), (1,)), ((), ())), preferred_element_type=jnp.float32
    )
    summed = lax.psum_scatter(
        partial_value.astype(jnp.bfloat16), "mp", scatter_dimension=1, tiled=True
    ).astype(jnp.float32)
    stream = residual.astype(jnp.float32) + summed
    gain_part = lax.dynamic_slice_in_dim(norm_gain, offset, shard_width, 0)
    factor_f = right_cols.astype(jnp.float32)
    crossed = jnp.dot(stream, factor_f.T, precision=lax.Precision.HIGHEST)
    per_token = jnp.sum(stream * stream, axis=1)
    per_member = jnp.sum(factor_f * factor_f, axis=1)
    projected, crossed, per_token, per_member = lax.psum(
        (projected, crossed, per_token, per_member), "mp"
    )
    lifted = factor * projected
    meansq = (
        per_token[:, None] + 2.0 * lifted * crossed + lifted * lifted * per_member[None, :]
    ) / full_width
    inverse = lax.rsqrt(meansq + EPSILON)
    local_error = error_sums(
        stream, lifted, factor_f, gain_part, target.astype(jnp.float32), inverse
    )
    member_total = lax.psum(local_error, "mp")
    fitness = -member_total / (tok_count * full_width)
    everyone = lax.all_gather(fitness, "pop", axis=0, tiled=True)
    count_all = everyone.shape[0]
    average = jnp.mean(everyone)
    centre = everyone - average
    spread = jnp.sqrt(jnp.mean(centre * centre) + 1e-05)
    weight = utility(member_ranks, count_all) + (fitness - average) / spread / count_all
    weighted = (weight[:, None] * left_factors.astype(jnp.float32)).astype(jnp.bfloat16)
    weighted_rows = lax.all_to_all(weighted, "pop", split_axis=1, concat_axis=0, tiled=True)
    right_all = lax.all_gather(right_cols, "pop", axis=0, tiled=True)
    update = lax.dot_general(
        weighted_rows, right_all, (((0,), (0,)), ((), ())), preferred_element_type=jnp.float32
    ) * (math.sqrt(count_all) / SIGMA)
    return (update, fitness, stream)


BLK = 256
F32 = jnp.float32
BF = jnp.bfloat16


def nt_dot(a, b):
    return lax.dot_general(a, b, (((1,), (1,)), ((), ())), preferred_element_type=F32)


def split_two(x):
    hi = x.astype(BF)
    return hi, (x - hi.astype(F32)).astype(BF)


def row_sums(ones, acc):
    hi = acc.astype(BF)
    rest = acc - hi.astype(F32)
    mid, low = split_two(rest)
    return nt_dot(ones, hi) + nt_dot(ones, mid) + nt_dot(ones, low)


def fold_lanes(x):
    total = x[:, :128]
    for i in range(1, x.shape[1] // 128):
        total = total + x[:, i * 128:(i + 1) * 128]
    return total


def kernel(
    n_pop, n_mp, ctx_h, w_h, res_h, tgt_h, gain_h, left_h, right_h, ranks_h,
    base, weighted, right_all, fit_out,
    w_v, ctx, res, tgt, lcols, gain, right, ranks, send_a, recv_a, send_y, recv_y, send_b, recv_b,
    lall, rall, uall, mixed, sq_s, sq_a, sq_e, pre, pre_in, post, post_in, fits,
    w_sem, loc_sem, sa, ra, sy, ry, sb, rb, s_pre, r_pre, s_post, r_post,
    s_l, r_l, s_r, r_r, s_u, r_u, s_f, r_f,
):
    tok, width = ctx.shape
    mem = right.shape[0]
    full = right.shape[1]
    rows = full // n_pop
    chunks = width // BLK
    quarter = tok // n_mp
    members = mem * n_pop
    p = lax.axis_index("pop")
    q = lax.axis_index("mp")
    y = q // 2
    c = q % 2
    mate = y * 2 + (1 - c)
    across = (1 - y) * 2 + c
    diagonal = (1 - y) * 2 + (1 - c)
    blocks = (diagonal, across, mate, q)

    def remote(src, dst, ss, rs, pop, mp):
        return pltpu.make_async_remote_copy(
            src_ref=src, dst_ref=dst, send_sem=ss, recv_sem=rs,
            device_id=(pop, mp), device_id_type=pl.DeviceIdType.MESH,
        )

    def w_copy(s, k):
        start = pl.multiple_of(blocks[s] * width + k * BLK, BLK)
        return pltpu.make_async_copy(w_h.at[:, pl.ds(start, BLK)], w_v.at[s, k], w_sem.at[s, k])

    my_cols = pl.ds(pl.multiple_of(q * width, BLK), width)
    my_rows = pl.ds(pl.multiple_of(p * rows, 128), rows)
    locals_ = [
        pltpu.make_async_copy(ctx_h, ctx, loc_sem.at[0]),
        pltpu.make_async_copy(res_h, res, loc_sem.at[1]),
        pltpu.make_async_copy(tgt_h, tgt, loc_sem.at[2]),
        pltpu.make_async_copy(left_h.at[:, my_cols], lcols, loc_sem.at[3]),
        pltpu.make_async_copy(left_h.at[:, my_rows], lall.at[0], loc_sem.at[4]),
        pltpu.make_async_copy(right_h.at[:, my_cols], rall.at[0], loc_sem.at[5]),
        pltpu.make_async_copy(gain_h, gain, loc_sem.at[6]),
        pltpu.make_async_copy(right_h, right, loc_sem.at[7]),
        pltpu.make_async_copy(ranks_h, ranks, loc_sem.at[8]),
    ]
    w_copy(0, 0).start()
    locals_[0].start()
    w_copy(1, 0).start()

    barrier = pltpu.get_barrier_semaphore()
    peers = [(i, j) for i in range(n_pop) for j in range(n_mp)][1:]
    for i, j in peers:
        pl.semaphore_signal(
            barrier, inc=1, device_id=((p + i) % n_pop, (q + j) % n_mp), device_id_type=pl.DeviceIdType.MESH
        )

    def copy_a(k):
        return remote(send_a.at[k], recv_a.at[k], sa.at[k], ra.at[k], p, mate)

    def copy_y(k):
        return remote(send_y.at[k], recv_y.at[k], sy.at[k], ry.at[k], p, across)

    def copy_b(k):
        return remote(send_b.at[k], recv_b.at[k], sb.at[k], rb.at[k], p, mate)

    def copy_l(d):
        peer = (p + d) % n_pop
        cols = pl.ds(pl.multiple_of(peer * rows, 128), rows)
        return remote(left_h.at[:, cols], lall.at[d], s_l.at[d - 1], r_l.at[d - 1], peer, q)

    def copy_r(d):
        return remote(right_h.at[:, my_cols], rall.at[d], s_r.at[d - 1], r_r.at[d - 1], (p + d) % n_pop, q)

    def copy_u(d):
        return remote(uall.at[0], uall.at[d], s_u.at[d - 1], r_u.at[d - 1], (p + d) % n_pop, q)

    def copy_f(i, j):
        n = i * n_mp + j - 1
        return remote(fits.at[0, q], fits.at[i, q], s_f.at[n], r_f.at[n], (p + i) % n_pop, (q + j) % n_mp)

    def arrive_f(i, j):
        n = i * n_mp + j - 1
        source = (q + n_mp - j) % n_mp
        return remote(fits.at[i, source], fits.at[i, source], s_f.at[n], r_f.at[n], (p + n_pop - i) % n_pop, source)

    def copy_pre(d):
        peer = (q + d) % n_mp
        return remote(pre.at[peer], pre_in.at[d - 1], s_pre.at[d - 1], r_pre.at[d - 1], p, peer)

    def copy_post(d):
        peer = (q + d) % n_mp
        return remote(post.at[peer], post_in.at[d - 1], s_post.at[d - 1], r_post.at[d - 1], p, peer)

    def product(s, k):
        w_copy(s, k).wait()
        return jnp.dot(ctx[...], w_v[s, k], preferred_element_type=F32)

    locals_[0].wait()
    w_copy(0, 0).wait()
    w_copy(0, 1).start()
    w_copy(2, 0).start()
    w_copy(1, 1).start()
    w_copy(2, 1).start()
    send_a[0] = jnp.dot(ctx[...], w_v[0, 0], preferred_element_type=F32).astype(BF)
    pl.semaphore_wait(barrier, n_mp * n_pop - 1)
    copy_a(0).start()

    def far(k, carry):
        @pl.when(k + 2 < chunks)
        def _():
            for s in range(3):
                w_copy(s, k + 2).start()

        w_copy(3, k).start()

        @pl.when(k == 1)
        def _():
            for item in locals_[1:]:
                item.start()

        mine = product(1, k)

        @pl.when(k + 1 < chunks)
        def _():
            send_a[k + 1] = product(0, k + 1).astype(BF)
            copy_a(k + 1).start()

        copy_a(k).wait_recv()
        send_y[k] = (mine + recv_a[k].astype(F32)).astype(BF)
        copy_y(k).start()
        send_b[k] = product(2, k).astype(BF)
        copy_b(k).start()
        return carry

    lax.fori_loop(0, chunks, far, 0)

    for item in locals_[1:]:
        item.wait()
    uall[0] = ranks[...].astype(F32)
    for d in range(1, n_pop):
        copy_l(d).start()
        copy_r(d).start()
        copy_u(d).start()

    def near(k, carry):
        cols = pl.ds(pl.multiple_of(k * BLK, BLK), BLK)
        base[:, cols] = product(3, k) + res[:, cols].astype(F32)
        return carry

    lax.fori_loop(0, chunks, near, 0)

    ones = jnp.ones((8, 128), BF)
    gain_mine = gain[:, my_cols]
    r_mine = rall[0].astype(F32)
    gr_hi, gr_lo = split_two(r_mine * gain_mine)
    for t in range(n_mp):
        part = slice(t * quarter, (t + 1) * quarter)
        target = tgt[part, :]
        pre[t, 0:mem, :] = nt_dot(lcols[...], ctx[part, :])
        pre[t, mem:2 * mem, :] = nt_dot(gr_hi, target) + nt_dot(gr_lo, target)
        wide = target.astype(F32)
        pre[t, 2 * mem:2 * mem + 8, :] = row_sums(ones, fold_lanes(wide * wide))
    for d in range(1, n_mp):
        copy_pre(d).start()
    g2_hi, g2_lo = split_two(r_mine * (gain_mine * gain_mine))
    for k in range(chunks):
        cols = slice(k * BLK, (k + 1) * BLK)
        mixed[k, 0:mem, :] = rall[0, :, cols]
        mixed[k, mem:2 * mem, :] = g2_hi[:, cols]
        mixed[k, 2 * mem:3 * mem, :] = g2_lo[:, cols]
    r_full = right[...].astype(F32)
    gr_full = r_full * gain[...]
    norm_r = jnp.sum(r_full * r_full, axis=1, keepdims=True)
    norm_gr = jnp.sum(gr_full * gr_full, axis=1, keepdims=True)
    sq_s[...] = jnp.zeros_like(sq_s)
    sq_a[...] = jnp.zeros_like(sq_a)
    sq_e[...] = jnp.zeros_like(sq_e)
    post[...] = jnp.zeros_like(post)

    def settle(k, carry):
        copy_b(k).wait_recv()
        copy_y(k).wait_recv()
        cols = pl.ds(pl.multiple_of(k * BLK, BLK), BLK)
        gain_k = gain[:, pl.ds(pl.multiple_of(q * width + k * BLK, BLK), BLK)]
        for t in range(n_mp):
            part = slice(t * quarter, (t + 1) * quarter)
            s = base[part, cols] + recv_b[k, part, :].astype(F32) + recv_y[k, part, :].astype(F32)
            base[part, cols] = s
            hi, low = split_two(s)
            both = nt_dot(mixed[k], hi) + nt_dot(mixed[k], low)
            post[t, 0:mem, :] += both[0:mem]
            post[t, mem:2 * mem, :] += both[mem:2 * mem] + both[2 * mem:3 * mem]
            gs = s * gain_k
            sq_s[part, :] += fold_lanes(s * s)
            sq_a[part, :] += fold_lanes(gs * gs)
            sq_e[part, :] += fold_lanes(gs * tgt[part, cols].astype(F32))
        return carry

    lax.fori_loop(0, chunks, settle, 0)
    line = lax.broadcasted_iota(jnp.int32, (8, quarter), 0)
    for t in range(n_mp):
        part = slice(t * quarter, (t + 1) * quarter)
        rest = jnp.where(line == 1, row_sums(ones, sq_a[part, :]), row_sums(ones, sq_e[part, :]))
        post[t, 2 * mem:2 * mem + 8, :] = jnp.where(line == 0, row_sums(ones, sq_s[part, :]), rest)
    for d in range(1, n_mp):
        copy_post(d).start()
    early = pre[q]
    for d in range(1, n_mp):
        copy_pre(d).wait_recv()
        early = early + pre_in[d - 1]
    late = post[q]
    for d in range(1, n_mp):
        copy_post(d).wait_recv()
        late = late + post_in[d - 1]
    lifted = early[0:mem] * (SIGMA / math.sqrt(full))
    cross_t = early[mem:2 * mem]
    t_sq = early[2 * mem:2 * mem + 1]
    crossed = late[0:mem]
    crossed_g = late[mem:2 * mem]
    s_sq = late[2 * mem:2 * mem + 1]
    a_sq = late[2 * mem + 1:2 * mem + 2]
    e_sq = late[2 * mem + 2:2 * mem + 3]
    meansq = (s_sq + 2.0 * lifted * crossed + lifted * lifted * norm_r) / full
    inverse = lax.rsqrt(meansq + EPSILON)
    power = a_sq + 2.0 * lifted * crossed_g + lifted * lifted * norm_gr
    errors = inverse * inverse * power - 2.0 * inverse * (e_sq + lifted * cross_t) + t_sq
    fits[0, q] = row_sums(jnp.ones((8, quarter), BF), errors)[0:1]
    for i, j in peers:
        copy_f(i, j).start()
    for d in range(1, n_pop):
        copy_l(d).wait_recv()
        copy_r(d).wait_recv()
        copy_u(d).wait_recv()
    for d in range(n_pop):
        right_all[d * mem:(d + 1) * mem, :] = rall[d]
    ceiling = math.log(members / 2 + 1)
    whole = sum(max(0.0, ceiling - math.log(i + 1.0)) for i in range(members))
    shaped = jnp.maximum(0.0, ceiling - jnp.log(uall[...] + 1.0)) / whole - 1.0 / members
    for i, j in peers:
        arrive_f(i, j).wait_recv()
    total = fits[:, 0]
    for j in range(1, n_mp):
        total = total + fits[:, j]
    everyone = -total / (tok * full)
    fit_out[...] = everyone[0]
    average = jnp.sum(jnp.sum(everyone, axis=0), axis=1, keepdims=True) / members
    centre = everyone - average[None]
    spread = jnp.sqrt(jnp.sum(jnp.sum(centre * centre, axis=0), axis=1, keepdims=True) / members + 1e-05)
    weight = shaped + centre / spread[None] / members
    square = (mem, mem)
    eye = lax.broadcasted_iota(jnp.int32, square, 0) == lax.broadcasted_iota(jnp.int32, square, 1)
    for d in range(n_pop):
        upright = jnp.sum(jnp.where(eye, weight[d], 0.0), axis=1, keepdims=True)
        weighted[d * mem:(d + 1) * mem, :] = (upright * lall[d].astype(F32)).astype(BF)

    def drain(k, carry):
        copy_a(k).wait_send()
        copy_y(k).wait_send()
        copy_b(k).wait_send()
        return carry

    lax.fori_loop(0, chunks, drain, 0)
    for d in range(1, n_mp):
        copy_pre(d).wait_send()
        copy_post(d).wait_send()
    for d in range(1, n_pop):
        copy_l(d).wait_send()
        copy_r(d).wait_send()
        copy_u(d).wait_send()
    for i, j in peers:
        copy_f(i, j).wait_send()


def in_hbm(x):
    return pltpu.with_memory_space_constraint(x, pltpu.HBM)


def fused_shards(
    n_pop, n_mp, context, out_weight, residual, target, norm_gain, left_factors, right_factors, member_ranks
):
    tok, width = context.shape
    full = out_weight.shape[1]
    mem = left_factors.shape[0]
    rows = full // n_pop
    chunks = width // BLK
    quarter = tok // n_mp
    ranks = member_ranks.reshape(1, mem)
    anywhere = pl.BlockSpec(memory_space=pltpu.HBM)
    vmem = pl.BlockSpec(memory_space=pltpu.VMEM)
    block = pltpu.VMEM((chunks, tok, BLK), BF)
    dma = pltpu.SemaphoreType.DMA
    acc = pltpu.VMEM((tok, 128), F32)
    base, weighted, right_all, fitness = pl.pallas_call(
        functools.partial(kernel, n_pop, n_mp),
        name="es_step",
        out_shape=(
            jax.ShapeDtypeStruct((tok, width), F32),
            jax.ShapeDtypeStruct((n_pop * mem, rows), BF),
            jax.ShapeDtypeStruct((n_pop * mem, width), BF),
            jax.ShapeDtypeStruct((1, mem), F32),
        ),
        in_specs=[anywhere] * 8,
        out_specs=[vmem] * 4,
        scratch_shapes=[
            pltpu.VMEM((4, chunks, width, BLK), BF),
            pltpu.VMEM((tok, width), BF),
            pltpu.VMEM((tok, width), BF),
            pltpu.VMEM((tok, width), BF),
            pltpu.VMEM((mem, width), BF),
            pltpu.VMEM((1, full), F32),
            pltpu.VMEM((mem, full), BF),
            pltpu.VMEM((1, mem), jnp.int32),
            block, block, block, block, block, block,
            pltpu.VMEM((n_pop, mem, rows), BF),
            pltpu.VMEM((n_pop, mem, width), BF),
            pltpu.VMEM((n_pop, 1, mem), F32),
            pltpu.VMEM((chunks, 3 * mem, BLK), BF),
            acc, acc, acc,
            pltpu.VMEM((n_mp, 2 * mem + 8, quarter), F32),
            pltpu.VMEM((n_mp - 1, 2 * mem + 8, quarter), F32),
            pltpu.VMEM((n_mp, 2 * mem + 8, quarter), F32),
            pltpu.VMEM((n_mp - 1, 2 * mem + 8, quarter), F32),
            pltpu.VMEM((n_pop, n_mp, 1, mem), F32),
            dma((4, chunks)),
            dma((9,)),
        ]
        + [dma((chunks,))] * 6
        + [dma((n_mp - 1,))] * 4
        + [dma((n_pop - 1,))] * 6
        + [dma((n_mp * n_pop - 1,))] * 2,
        compiler_params=pltpu.CompilerParams(
            collective_id=0, has_side_effects=True, vmem_limit_bytes=48 * 1024 * 1024
        ),
    )(
        *map(in_hbm, (
            context, out_weight, residual, target, norm_gain.reshape(1, full), left_factors,
            right_factors, ranks,
        ))
    )
    count_all = n_pop * mem
    update, base, fitness = pl.pallas_call(
        functools.partial(finish, math.sqrt(count_all) / SIGMA),
        name="es_update",
        out_shape=(
            jax.ShapeDtypeStruct((rows, width), F32),
            jax.ShapeDtypeStruct((tok, width), F32),
            jax.ShapeDtypeStruct((1, mem), F32),
        ),
        in_specs=[vmem] * 4,
        out_specs=[anywhere] * 3,
        scratch_shapes=[pltpu.VMEM((rows, width), F32), dma((rows // 128 + 2,))],
        compiler_params=pltpu.CompilerParams(vmem_limit_bytes=16 * 1024 * 1024),
    )(weighted, right_all, base, fitness)
    return (update, fitness.reshape(mem), base)


def finish(scale, weighted, right_all, base_in, fit_in, update, base, fit, held, sems):
    steps = held.shape[0] // 128
    copies = [
        pltpu.make_async_copy(base_in, base, sems.at[steps]),
        pltpu.make_async_copy(fit_in, fit, sems.at[steps + 1]),
    ]
    copies[0].start()
    copies[1].start()
    for i in range(steps):
        part = slice(i * 128, (i + 1) * 128)
        held[part, :] = lax.dot_general(
            weighted[:, part], right_all[...], (((0,), (0,)), ((), ())), preferred_element_type=F32
        ) * scale
        copies.append(pltpu.make_async_copy(held.at[part], update.at[part], sems.at[i]))
        copies[-1].start()
    for item in copies:
        item.wait()


def chosen(n_pop, n_mp, context, out_weight, *rest):
    tok, width = context.shape
    mem = rest[3].shape[0]
    full = out_weight.shape[1]
    if n_mp == 4 and width % BLK == 0 and width > BLK and (full // n_pop) % 128 == 0 and tok % (16 * n_mp) == 0 and mem % 16 == 0:
        return fused_shards(n_pop, n_mp, context, out_weight, *rest)
    return shards(context, out_weight, *rest)


def solution(mesh):
    in_specs = (
        P("pop", "mp"),
        P("mp", None),
        P("pop", "mp"),
        P("pop", "mp"),
        P(),
        P("pop", None),
        P("pop", None),
        P("pop"),
    )
    out_specs = (P("pop", "mp"), P("pop"), P("pop", "mp"))
    return jax.shard_map(
        functools.partial(chosen, mesh.shape["pop"], mesh.shape["mp"]), mesh=mesh, in_specs=in_specs, out_specs=out_specs, check_vma=False)
```

```python
import functools
import math

import jax
import jax.numpy as jnp
from jax import lax
from jax.experimental import pallas as pl
from jax.experimental.pallas import tpu as pltpu
from jax.sharding import PartitionSpec as P

SIGMA = 1.0
EPSILON = 1e-06


def error_sums(stream, lifted, right_rows, gain_part, target_rows, inverse):
    hidden = stream[:, None, :] + lifted[:, :, None] * right_rows[None, :, :]
    differ = gain_part * hidden * inverse[:, :, None] - target_rows[:, None, :]
    return jnp.sum(differ * differ, axis=(0, 2))


def utility(member_ranks, count_all):
    levels = jnp.arange(count_all).astype(jnp.float32)
    ceiling = math.log(count_all / 2 + 1)
    baseline = jnp.maximum(0.0, ceiling - jnp.log(levels + 1.0))
    shaped = jnp.maximum(0.0, ceiling - jnp.log(member_ranks.astype(jnp.float32) + 1.0))
    return shaped / jnp.sum(baseline) - 1.0 / count_all


def shards(
    context, out_weight, residual, target, norm_gain, left_factors, right_factors, member_ranks
):
    tok_count = context.shape[0]
    shard_width = context.shape[1]
    full_width = out_weight.shape[1]
    factor = SIGMA / math.sqrt(full_width)
    offset = lax.axis_index("mp") * shard_width
    left_cols = lax.dynamic_slice_in_dim(left_factors, offset, shard_width, 1)
    right_cols = lax.dynamic_slice_in_dim(right_factors, offset, shard_width, 1)
    partial_value = jnp.dot(context, out_weight, preferred_element_type=jnp.float32)
    projected = lax.dot_general(
        context, left_cols, (((1,), (1,)), ((), ())), preferred_element_type=jnp.float32
    )
    summed = lax.psum_scatter(
        partial_value.astype(jnp.bfloat16), "mp", scatter_dimension=1, tiled=True
    ).astype(jnp.float32)
    stream = residual.astype(jnp.float32) + summed
    gain_part = lax.dynamic_slice_in_dim(norm_gain, offset, shard_width, 0)
    factor_f = right_cols.astype(jnp.float32)
    crossed = jnp.dot(stream, factor_f.T, precision=lax.Precision.HIGHEST)
    per_token = jnp.sum(stream * stream, axis=1)
    per_member = jnp.sum(factor_f * factor_f, axis=1)
    projected, crossed, per_token, per_member = lax.psum(
        (projected, crossed, per_token, per_member), "mp"
    )
    lifted = factor * projected
    meansq = (
        per_token[:, None] + 2.0 * lifted * crossed + lifted * lifted * per_member[None, :]
    ) / full_width
    inverse = lax.rsqrt(meansq + EPSILON)
    local_error = error_sums(
        stream, lifted, factor_f, gain_part, target.astype(jnp.float32), inverse
    )
    member_total = lax.psum(local_error, "mp")
    fitness = -member_total / (tok_count * full_width)
    everyone = lax.all_gather(fitness, "pop", axis=0, tiled=True)
    count_all = everyone.shape[0]
    average = jnp.mean(everyone)
    centre = everyone - average
    spread = jnp.sqrt(jnp.mean(centre * centre) + 1e-05)
    weight = utility(member_ranks, count_all) + (fitness - average) / spread / count_all
    weighted = (weight[:, None] * left_factors.astype(jnp.float32)).astype(jnp.bfloat16)
    weighted_rows = lax.all_to_all(weighted, "pop", split_axis=1, concat_axis=0, tiled=True)
    right_all = lax.all_gather(right_cols, "pop", axis=0, tiled=True)
    update = lax.dot_general(
        weighted_rows, right_all, (((0,), (0,)), ((), ())), preferred_element_type=jnp.float32
    ) * (math.sqrt(count_all) / SIGMA)
    return (update, fitness, stream)


BLK = 256
F32 = jnp.float32
BF = jnp.bfloat16


def nt_dot(a, b):
    return lax.dot_general(a, b, (((1,), (1,)), ((), ())), preferred_element_type=F32)


def split_two(x):
    hi = x.astype(BF)
    return hi, (x - hi.astype(F32)).astype(BF)


def row_sums(ones, acc):
    hi = acc.astype(BF)
    rest = acc - hi.astype(F32)
    mid, low = split_two(rest)
    return nt_dot(ones, hi) + nt_dot(ones, mid) + nt_dot(ones, low)


def fold_lanes(x):
    total = x[:, :128]
    for i in range(1, x.shape[1] // 128):
        total = total + x[:, i * 128:(i + 1) * 128]
    return total


def kernel(
    n_pop, n_mp, ctx_h, w_h, res_h, tgt_h, gain_h, left_h, right_h, ranks_h,
    base, weighted, right_all, fit_out,
    w_v, ctx, res, tgt, lcols, gain, right, ranks, send_a, recv_a, send_y, recv_y, send_b, recv_b,
    lall, rall, uall, mixed, sq_s, sq_a, sq_e, pre, pre_in, post, post_in, fits,
    w_sem, loc_sem, sa, ra, sy, ry, sb, rb, s_pre, r_pre, s_post, r_post,
    s_l, r_l, s_r, r_r, s_u, r_u, s_f, r_f,
):
    tok, width = ctx.shape
    mem = right.shape[0]
    full = right.shape[1]
    rows = full // n_pop
    chunks = width // BLK
    quarter = tok // n_mp
    members = mem * n_pop
    p = lax.axis_index("pop")
    q = lax.axis_index("mp")
    y = q // 2
    c = q % 2
    mate = y * 2 + (1 - c)
    across = (1 - y) * 2 + c
    diagonal = (1 - y) * 2 + (1 - c)
    blocks = (diagonal, across, mate, q)

    def remote(src, dst, ss, rs, pop, mp):
        return pltpu.make_async_remote_copy(
            src_ref=src, dst_ref=dst, send_sem=ss, recv_sem=rs,
            device_id=(pop, mp), device_id_type=pl.DeviceIdType.MESH,
        )

    def w_copy(s, k):
        start = pl.multiple_of(blocks[s] * width + k * BLK, BLK)
        return pltpu.make_async_copy(w_h.at[:, pl.ds(start, BLK)], w_v.at[s, k], w_sem.at[s, k])

    my_cols = pl.ds(pl.multiple_of(q * width, BLK), width)
    my_rows = pl.ds(pl.multiple_of(p * rows, 128), rows)
    locals_ = [
        pltpu.make_async_copy(ctx_h, ctx, loc_sem.at[0]),
        pltpu.make_async_copy(res_h, res, loc_sem.at[1]),
        pltpu.make_async_copy(tgt_h, tgt, loc_sem.at[2]),
        pltpu.make_async_copy(left_h.at[:, my_cols], lcols, loc_sem.at[3]),
        pltpu.make_async_copy(left_h.at[:, my_rows], lall.at[0], loc_sem.at[4]),
        pltpu.make_async_copy(right_h.at[:, my_cols], rall.at[0], loc_sem.at[5]),
        pltpu.make_async_copy(gain_h, gain, loc_sem.at[6]),
        pltpu.make_async_copy(right_h, right, loc_sem.at[7]),
        pltpu.make_async_copy(ranks_h, ranks, loc_sem.at[8]),
    ]
    w_copy(0, 0).start()
    locals_[0].start()
    w_copy(1, 0).start()

    barrier = pltpu.get_barrier_semaphore()
    peers = [(i, j) for i in range(n_pop) for j in range(n_mp)][1:]
    for i, j in peers:
        pl.semaphore_signal(
            barrier, inc=1, device_id=((p + i) % n_pop, (q + j) % n_mp), device_id_type=pl.DeviceIdType.MESH
        )

    def copy_a(k):
        return remote(send_a.at[k], recv_a.at[k], sa.at[k], ra.at[k], p, mate)

    def copy_y(k):
        return remote(send_y.at[k], recv_y.at[k], sy.at[k], ry.at[k], p, across)

    def copy_b(k):
        return remote(send_b.at[k], recv_b.at[k], sb.at[k], rb.at[k], p, mate)

    def copy_l(d):
        peer = (p + d) % n_pop
        cols = pl.ds(pl.multiple_of(peer * rows, 128), rows)
        return remote(left_h.at[:, cols], lall.at[d], s_l.at[d - 1], r_l.at[d - 1], peer, q)

    def copy_r(d):
        return remote(right_h.at[:, my_cols], rall.at[d], s_r.at[d - 1], r_r.at[d - 1], (p + d) % n_pop, q)

    def copy_u(d):
        return remote(uall.at[0], uall.at[d], s_u.at[d - 1], r_u.at[d - 1], (p + d) % n_pop, q)

    def copy_f(i, j):
        n = i * n_mp + j - 1
        return remote(fits.at[0, q], fits.at[i, q], s_f.at[n], r_f.at[n], (p + i) % n_pop, (q + j) % n_mp)

    def arrive_f(i, j):
        n = i * n_mp + j - 1
        source = (q + n_mp - j) % n_mp
        return remote(fits.at[i, source], fits.at[i, source], s_f.at[n], r_f.at[n], (p + n_pop - i) % n_pop, source)

    def copy_pre(d):
        peer = (q + d) % n_mp
        return remote(pre.at[peer], pre_in.at[d - 1], s_pre.at[d - 1], r_pre.at[d - 1], p, peer)

    def copy_post(d):
        peer = (q + d) % n_mp
        return remote(post.at[peer], post_in.at[d - 1], s_post.at[d - 1], r_post.at[d - 1], p, peer)

    def product(s, k):
        w_copy(s, k).wait()
        return jnp.dot(ctx[...], w_v[s, k], preferred_element_type=F32)

    locals_[0].wait()
    w_copy(0, 0).wait()
    w_copy(0, 1).start()
    w_copy(2, 0).start()
    w_copy(1, 1).start()
    w_copy(2, 1).start()
    send_a[0] = jnp.dot(ctx[...], w_v[0, 0], preferred_element_type=F32).astype(BF)
    pl.semaphore_wait(barrier, n_mp * n_pop - 1)
    copy_a(0).start()

    def far(k, carry):
        @pl.when(k + 2 < chunks)
        def _():
            for s in range(3):
                w_copy(s, k + 2).start()

        w_copy(3, k).start()

        @pl.when(k == 1)
        def _():
            for item in locals_[1:]:
                item.start()

        mine = product(1, k)

        @pl.when(k + 1 < chunks)
        def _():
            send_a[k + 1] = product(0, k + 1).astype(BF)
            copy_a(k + 1).start()

        copy_a(k).wait_recv()
        send_y[k] = (mine + recv_a[k].astype(F32)).astype(BF)
        copy_y(k).start()
        send_b[k] = product(2, k).astype(BF)
        copy_b(k).start()
        return carry

    lax.fori_loop(0, chunks, far, 0)

    for item in locals_[1:]:
        item.wait()
    uall[0] = ranks[...].astype(F32)
    for d in range(1, n_pop):
        copy_l(d).start()
        copy_r(d).start()
        copy_u(d).start()

    def near(k, carry):
        cols = pl.ds(pl.multiple_of(k * BLK, BLK), BLK)
        base[:, cols] = product(3, k) + res[:, cols].astype(F32)
        return carry

    lax.fori_loop(0, chunks, near, 0)

    ones = jnp.ones((8, 128), BF)
    gain_mine = gain[:, my_cols]
    r_mine = rall[0].astype(F32)
    gr_hi, gr_lo = split_two(r_mine * gain_mine)
    squares = jnp.zeros((quarter, 128), F32)
    for t in range(n_mp):
        part = slice(t * quarter, (t + 1) * quarter)
        target = tgt[part, :]
        pre[t, 0:mem, :] = nt_dot(lcols[...], ctx[part, :])
        pre[t, mem:2 * mem, :] = nt_dot(gr_hi, target) + nt_dot(gr_lo, target)
        wide = target.astype(F32)
        squares = squares + fold_lanes(wide * wide)
    for d in range(1, n_mp):
        copy_pre(d).start()
    t_sq = jnp.sum(jnp.sum(squares, axis=1, keepdims=True), axis=0, keepdims=True)
    g2_hi, g2_lo = split_two(r_mine * (gain_mine * gain_mine))
    for k in range(chunks):
        cols = slice(k * BLK, (k + 1) * BLK)
        mixed[k, 0:mem, :] = rall[0, :, cols]
        mixed[k, mem:2 * mem, :] = g2_hi[:, cols]
        mixed[k, 2 * mem:3 * mem, :] = g2_lo[:, cols]
    r_full = right[...].astype(F32)
    gr_full = r_full * gain[...]
    norm_r = jnp.sum(r_full * r_full, axis=1, keepdims=True)
    norm_gr = jnp.sum(gr_full * gr_full, axis=1, keepdims=True)
    sq_s[...] = jnp.zeros_like(sq_s)
    sq_a[...] = jnp.zeros_like(sq_a)
    sq_e[...] = jnp.zeros_like(sq_e)
    post[...] = jnp.zeros_like(post)

    def settle(k, carry):
        copy_b(k).wait_recv()
        copy_y(k).wait_recv()
        cols = pl.ds(pl.multiple_of(k * BLK, BLK), BLK)
        gain_k = gain[:, pl.ds(pl.multiple_of(q * width + k * BLK, BLK), BLK)]
        for t in range(n_mp):
            part = slice(t * quarter, (t + 1) * quarter)
            s = base[part, cols] + recv_b[k, part, :].astype(F32) + recv_y[k, part, :].astype(F32)
            base[part, cols] = s
            hi, low = split_two(s)
            both = nt_dot(mixed[k], hi) + nt_dot(mixed[k], low)
            post[t, 0:mem, :] += both[0:mem]
            post[t, mem:2 * mem, :] += both[mem:2 * mem] + both[2 * mem:3 * mem]
            gs = s * gain_k
            sq_s[part, :] += fold_lanes(s * s)
            sq_a[part, :] += fold_lanes(gs * gs)
            sq_e[part, :] += fold_lanes(gs * tgt[part, cols].astype(F32))
        return carry

    lax.fori_loop(0, chunks, settle, 0)
    line = lax.broadcasted_iota(jnp.int32, (8, quarter), 0)
    for t in range(n_mp):
        part = slice(t * quarter, (t + 1) * quarter)
        rest = jnp.where(line == 1, row_sums(ones, sq_a[part, :]), row_sums(ones, sq_e[part, :]))
        post[t, 2 * mem:2 * mem + 8, :] = jnp.where(line == 0, row_sums(ones, sq_s[part, :]), rest)
    for d in range(1, n_mp):
        copy_post(d).start()
    early = pre[q]
    for d in range(1, n_mp):
        copy_pre(d).wait_recv()
        early = early + pre_in[d - 1]
    late = post[q]
    for d in range(1, n_mp):
        copy_post(d).wait_recv()
        late = late + post_in[d - 1]
    lifted = early[0:mem] * (SIGMA / math.sqrt(full))
    cross_t = early[mem:2 * mem]
    crossed = late[0:mem]
    crossed_g = late[mem:2 * mem]
    s_sq = late[2 * mem:2 * mem + 1]
    a_sq = late[2 * mem + 1:2 * mem + 2]
    e_sq = late[2 * mem + 2:2 * mem + 3]
    meansq = (s_sq + 2.0 * lifted * crossed + lifted * lifted * norm_r) / full
    inverse = lax.rsqrt(meansq + EPSILON)
    power = a_sq + 2.0 * lifted * crossed_g + lifted * lifted * norm_gr
    errors = inverse * inverse * power - 2.0 * inverse * (e_sq + lifted * cross_t)
    fits[0, q] = row_sums(jnp.ones((8, quarter), BF), errors)[0:1] + t_sq
    for i, j in peers:
        copy_f(i, j).start()
    for d in range(1, n_pop):
        copy_l(d).wait_recv()
        copy_r(d).wait_recv()
        copy_u(d).wait_recv()
    for d in range(n_pop):
        right_all[d * mem:(d + 1) * mem, :] = rall[d]
    ceiling = math.log(members / 2 + 1)
    whole = sum(max(0.0, ceiling - math.log(i + 1.0)) for i in range(members))
    shaped = jnp.maximum(0.0, ceiling - jnp.log(uall[...] + 1.0)) / whole - 1.0 / members
    for i, j in peers:
        arrive_f(i, j).wait_recv()
    total = fits[:, 0]
    for j in range(1, n_mp):
        total = total + fits[:, j]
    everyone = -total / (tok * full)
    fit_out[...] = everyone[0]
    average = jnp.sum(jnp.sum(everyone, axis=0), axis=1, keepdims=True) / members
    centre = everyone - average[None]
    spread = jnp.sqrt(jnp.sum(jnp.sum(centre * centre, axis=0), axis=1, keepdims=True) / members + 1e-05)
    weight = shaped + centre / spread[None] / members
    square = (mem, mem)
    eye = lax.broadcasted_iota(jnp.int32, square, 0) == lax.broadcasted_iota(jnp.int32, square, 1)
    for d in range(n_pop):
        upright = jnp.sum(jnp.where(eye, weight[d], 0.0), axis=1, keepdims=True)
        weighted[d * mem:(d + 1) * mem, :] = (upright * lall[d].astype(F32)).astype(BF)

    def drain(k, carry):
        copy_a(k).wait_send()
        copy_y(k).wait_send()
        copy_b(k).wait_send()
        return carry

    lax.fori_loop(0, chunks, drain, 0)
    for d in range(1, n_mp):
        copy_pre(d).wait_send()
        copy_post(d).wait_send()
    for d in range(1, n_pop):
        copy_l(d).wait_send()
        copy_r(d).wait_send()
        copy_u(d).wait_send()
    for i, j in peers:
        copy_f(i, j).wait_send()


def in_hbm(x):
    return pltpu.with_memory_space_constraint(x, pltpu.HBM)


def fused_shards(
    n_pop, n_mp, context, out_weight, residual, target, norm_gain, left_factors, right_factors, member_ranks
):
    tok, width = context.shape
    full = out_weight.shape[1]
    mem = left_factors.shape[0]
    rows = full // n_pop
    chunks = width // BLK
    quarter = tok // n_mp
    ranks = member_ranks.reshape(1, mem)
    anywhere = pl.BlockSpec(memory_space=pltpu.HBM)
    vmem = pl.BlockSpec(memory_space=pltpu.VMEM)
    block = pltpu.VMEM((chunks, tok, BLK), BF)
    dma = pltpu.SemaphoreType.DMA
    acc = pltpu.VMEM((tok, 128), F32)
    base, weighted, right_all, fitness = pl.pallas_call(
        functools.partial(kernel, n_pop, n_mp),
        name="es_step",
        out_shape=(
            jax.ShapeDtypeStruct((tok, width), F32),
            jax.ShapeDtypeStruct((n_pop * mem, rows), BF),
            jax.ShapeDtypeStruct((n_pop * mem, width), BF),
            jax.ShapeDtypeStruct((1, mem), F32),
        ),
        in_specs=[anywhere] * 8,
        out_specs=[vmem] * 4,
        scratch_shapes=[
            pltpu.VMEM((4, chunks, width, BLK), BF),
            pltpu.VMEM((tok, width), BF),
            pltpu.VMEM((tok, width), BF),
            pltpu.VMEM((tok, width), BF),
            pltpu.VMEM((mem, width), BF),
            pltpu.VMEM((1, full), F32),
            pltpu.VMEM((mem, full), BF),
            pltpu.VMEM((1, mem), jnp.int32),
            block, block, block, block, block, block,
            pltpu.VMEM((n_pop, mem, rows), BF),
            pltpu.VMEM((n_pop, mem, width), BF),
            pltpu.VMEM((n_pop, 1, mem), F32),
            pltpu.VMEM((chunks, 3 * mem, BLK), BF),
            acc, acc, acc,
            pltpu.VMEM((n_mp, 2 * mem, quarter), F32),
            pltpu.VMEM((n_mp - 1, 2 * mem, quarter), F32),
            pltpu.VMEM((n_mp, 2 * mem + 8, quarter), F32),
            pltpu.VMEM((n_mp - 1, 2 * mem + 8, quarter), F32),
            pltpu.VMEM((n_pop, n_mp, 1, mem), F32),
            dma((4, chunks)),
            dma((9,)),
        ]
        + [dma((chunks,))] * 6
        + [dma((n_mp - 1,))] * 4
        + [dma((n_pop - 1,))] * 6
        + [dma((n_mp * n_pop - 1,))] * 2,
        compiler_params=pltpu.CompilerParams(
            collective_id=0, has_side_effects=True, vmem_limit_bytes=48 * 1024 * 1024
        ),
    )(
        *map(in_hbm, (
            context, out_weight, residual, target, norm_gain.reshape(1, full), left_factors,
            right_factors, ranks,
        ))
    )
    count_all = n_pop * mem
    update, base, fitness = pl.pallas_call(
        functools.partial(finish, math.sqrt(count_all) / SIGMA),
        name="es_update",
        out_shape=(
            jax.ShapeDtypeStruct((rows, width), F32),
            jax.ShapeDtypeStruct((tok, width), F32),
            jax.ShapeDtypeStruct((1, mem), F32),
        ),
        in_specs=[vmem] * 4,
        out_specs=[anywhere] * 3,
        scratch_shapes=[pltpu.VMEM((rows, width), F32), dma((rows // 128 + 2,))],
        compiler_params=pltpu.CompilerParams(vmem_limit_bytes=16 * 1024 * 1024),
    )(weighted, right_all, base, fitness)
    return (update, fitness.reshape(mem), base)


def finish(scale, weighted, right_all, base_in, fit_in, update, base, fit, held, sems):
    steps = held.shape[0] // 128
    copies = [
        pltpu.make_async_copy(base_in, base, sems.at[steps]),
        pltpu.make_async_copy(fit_in, fit, sems.at[steps + 1]),
    ]
    copies[0].start()
    copies[1].start()
    for i in range(steps):
        part = slice(i * 128, (i + 1) * 128)
        held[part, :] = lax.dot_general(
            weighted[:, part], right_all[...], (((0,), (0,)), ((), ())), preferred_element_type=F32
        ) * scale
        copies.append(pltpu.make_async_copy(held.at[part], update.at[part], sems.at[i]))
        copies[-1].start()
    for item in copies:
        item.wait()


def chosen(n_pop, n_mp, context, out_weight, *rest):
    tok, width = context.shape
    mem = rest[3].shape[0]
    full = out_weight.shape[1]
    if n_mp == 4 and width % BLK == 0 and width > BLK and (full // n_pop) % 128 == 0 and tok % (16 * n_mp) == 0 and mem % 16 == 0:
        return fused_shards(n_pop, n_mp, context, out_weight, *rest)
    return shards(context, out_weight, *rest)


def solution(mesh):
    in_specs = (
        P("pop", "mp"),
        P("mp", None),
        P("pop", "mp"),
        P("pop", "mp"),
        P(),
        P("pop", None),
        P("pop", None),
        P("pop"),
    )
    out_specs = (P("pop", "mp"), P("pop"), P("pop", "mp"))
    return jax.shard_map(
        functools.partial(chosen, mesh.shape["pop"], mesh.shape["mp"]), mesh=mesh, in_specs=in_specs, out_specs=out_specs, check_vma=False)
```
